128 devices in a mesh: group: 8 (over y, core), within: 16 (over z, x).
Axes of the slice: x: 4, y: 4, z: 4, core: 2. Of those that a mesh axis runs over, the one named last changes fastest.
Arguments:
- tokens: bfloat16 [16384, 2048], P(('group', 'within')), may hold values from -6 to 6
- languages: int32 [16384], P(('group', 'within')), may hold values from 0 to 99, as said below
- lang_group: int32 [100], replicated, may hold values from 0 to 7, as said below
- group_gain: float32 [8, 2048], replicated, may hold values from 0.25 to 1.75
- group_w1: bfloat16 [8, 2048, 8192], P('group', None, 'within'), may hold values from -0.125 to 0.125
- group_b1: float32 [8, 8192], P('group', 'within'), may hold values from -3 to 3
- group_w2: bfloat16 [8, 8192, 2048], P('group', 'within'), may hold values from -0.0625 to 0.0625
- group_b2: float32 [8, 2048], replicated, may hold values from -3 to 3
- shared_gain: float32 [2048], replicated, may hold values from 0.25 to 1.75
- shared_w1: bfloat16 [2048, 8192], P(None, 'group'), may hold values from -0.125 to 0.125
- shared_b1: float32 [8192], P('group'), may hold values from -3 to 3
- shared_w2: bfloat16 [8192, 2048], P('group'), may hold values from -0.0625 to 0.0625
- shared_b2: float32 [2048], replicated, may hold values from -3 to 3
Outputs:
- encoded: bfloat16 [16384, 2048], P(('group', 'within'))
The draws below stay inside these ranges and needn't reach their ends.
Inputs may be any that keep to these rules, and one draw needn't show every extreme that they name: `lang_group`: every language lies in one group and every group holds at least one language. Among the 128 tokens of one device (an aligned block), at most 24 have languages of one group, and in every block some group has exactly 24.
All inputs are finite; a program needn't handle non-finite values.
Results may differ from the reference program's by a relative error of at most 0.017.
Values may be sent and summed in bfloat16 or wider, within the bound.
No kernel may reach another device: no remote copies, remote signals or barrier semaphores. Data moves between devices by JAX's collectives and lax.ppermute only.
A program may use at most 128 MiB of HBM per device.

```python
import jax
import jax.numpy as jnp
from jax import lax

D = 2048
FF = 8192
LANGS = 100
TOK_DEV = 128
GROUPS = 8
CAP = 24
TOKENS = 16384
N_WITHIN = 16
DEVICES = 128


def joint_draw(key):
    ordering = jax.random.permutation(jax.random.fold_in(key, 11), LANGS).astype(jnp.int32)
    lang_table = jnp.zeros((LANGS,), jnp.int32).at[ordering].set((jnp.arange(LANGS, dtype=jnp.int32) % GROUPS).astype(jnp.int32))
    num_blocks = TOKENS // TOK_DEV
    favourite = jax.random.randint(jax.random.fold_in(key, 12), (), 0, GROUPS)
    coinflip = jax.random.randint(jax.random.fold_in(key, 13), (num_blocks,), 0, 4)
    others = jax.random.randint(jax.random.fold_in(key, 14), (num_blocks,), 0, GROUPS)
    hottest = jnp.where(coinflip < 3, favourite, others).astype(jnp.int32)
    position = jnp.arange(TOK_DEV, dtype=jnp.int32)
    remaining = (hottest[:, None] + 1 + (position[None, :] - CAP) % (GROUPS - 1)) % GROUPS
    group_rows = jnp.where(position[None, :] < CAP, hottest[:, None], remaining).astype(jnp.int32)
    block_keys = jax.random.split(jax.random.fold_in(key, 15), num_blocks)
    shuffles = jax.vmap(lambda single: jax.random.permutation(single, TOK_DEV))(block_keys).astype(jnp.int32)
    group_rows = jnp.take_along_axis(group_rows, shuffles, axis=1)
    group_sizes = (LANGS - group_rows + GROUPS - 1) // GROUPS
    first_pick = jax.random.randint(jax.random.fold_in(key, 16), group_rows.shape, 0, 1048576) % group_sizes
    second_pick = jax.random.randint(jax.random.fold_in(key, 17), group_rows.shape, 0, 1048576) % group_sizes
    chosen = jnp.minimum(first_pick, second_pick)
    language_ids = ordering[group_rows + GROUPS * chosen]
    return (lang_table, language_ids.reshape(TOKENS).astype(jnp.int32))


def draw_languages(key, part):
    return joint_draw(key)[1]


def draw_lang_group(key, part):
    return joint_draw(key)[0]


def shard_levels(own_key, shape, shards, low, high):
    def one(axis_at, blocks):
        steps = jax.random.uniform(jax.random.fold_in(jax.random.fold_in(own_key, 6), axis_at), (blocks,), jnp.float32, low / len(shards), high / len(shards))
        return jnp.repeat(jnp.exp(steps), shape[axis_at] // blocks).reshape((-1,) + (1,) * (len(shape) - axis_at - 1))

    factor_of = one(*shards[0])
    for cut in shards[1:]:
        factor_of = factor_of * one(*cut)
    return factor_of


def bell_draw(rng, shape, scale, bound, shards=(), held_as=jnp.bfloat16):
    drawn = jax.random.normal(rng, shape, jnp.float32) * scale
    if len(shards) > 0:
        drawn = shard_levels(rng, shape, shards, -0.22, 0.18) * drawn
    return jnp.clip(drawn, min=-bound, max=bound).astype(held_as)


def setup_inputs(seed: int = 0) -> dict:
    key_of = jax.random.split(jax.random.key(seed), 14)
    return {
        "tokens": bell_draw(key_of[0], (TOKENS, D), 1.0, 6.0, ((0, 128),)),
        "languages": draw_languages(jax.random.fold_in(key_of[13], 71), 0),
        "lang_group": draw_lang_group(jax.random.fold_in(key_of[13], 71), 0),
        "group_gain": jnp.clip(1.0 + 0.15 * jax.random.normal(key_of[3], (GROUPS, D), jnp.float32), 0.25, 1.75),
        "group_w1": bell_draw(key_of[4], (GROUPS, D, FF), D ** -0.5, 0.125, ((0, 8), (2, 16))),
        "group_b1": bell_draw(key_of[5], (GROUPS, FF), 0.5, 3.0, ((0, 8), (1, 16)), jnp.float32),
        "group_w2": bell_draw(key_of[6], (GROUPS, FF, D), FF ** -0.5, 0.0625, ((0, 8), (1, 16))),
        "group_b2": bell_draw(key_of[7], (GROUPS, D), 0.5, 3.0, (), jnp.float32),
        "shared_gain": jnp.clip(1.0 + 0.15 * jax.random.normal(key_of[8], (D,), jnp.float32), 0.25, 1.75),
        "shared_w1": bell_draw(key_of[9], (D, FF), D ** -0.5, 0.125, ((1, 8),)),
        "shared_b1": bell_draw(key_of[10], (FF,), 0.5, 3.0, ((0, 8),), jnp.float32),
        "shared_w2": bell_draw(key_of[11], (FF, D), FF ** -0.5, 0.0625, ((0, 8),)),
        "shared_b2": bell_draw(key_of[12], (D,), 0.5, 3.0, (), jnp.float32),
    }


def layer_norm(values, gains):
    centre = lax.optimization_barrier(jnp.mean(values, axis=-1, keepdims=True))
    centred = values - centre
    spread = lax.optimization_barrier(jnp.mean(centred * centred, axis=-1, keepdims=True))
    return centred * lax.rsqrt(spread + 1e-05) * gains

def reference(tokens, languages, lang_group, group_gain, group_w1, group_b1, group_w2, group_b2, shared_gain, shared_w1, shared_b1, shared_w2, shared_b2):
    residual_in = tokens.astype(jnp.float32)
    lang_hit = (languages[:, None] == jnp.arange(LANGS, dtype=jnp.int32)[None, :]).astype(jnp.int32)
    group_of = lax.optimization_barrier(jnp.sum(lang_hit * lang_group[None, :], axis=1)).astype(jnp.int32)
    onehot = (group_of[:, None] == jnp.arange(GROUPS, dtype=jnp.int32)[None, :]).astype(jnp.int32)
    blocks = onehot.reshape(DEVICES, TOK_DEV, GROUPS)
    earlier = jnp.cumsum(blocks, axis=1) - blocks
    slot_index = lax.optimization_barrier(jnp.sum(earlier * blocks, axis=2)).reshape(TOKENS).astype(jnp.int32)
    device = (jnp.arange(TOKENS, dtype=jnp.int32) // TOK_DEV).astype(jnp.int32)
    normed = layer_norm(residual_in, group_gain[group_of]).astype(jnp.bfloat16)
    position = (device * CAP + slot_index).astype(jnp.int32)
    unit_width = FF // N_WITHIN
    group_out = jnp.zeros((TOKENS, D), jnp.bfloat16)
    for group in range(GROUPS):
        member = group_of == group
        target = jnp.where(member, position, DEVICES * CAP).astype(jnp.int32)
        buffer = jnp.zeros((DEVICES * CAP, D), jnp.bfloat16).at[target].set(normed, mode='drop')
        hidden = jax.nn.relu(jnp.dot(buffer, group_w1[group], preferred_element_type=jnp.float32) + group_b1[group]).astype(jnp.bfloat16)
        accum_sum = jnp.zeros((DEVICES * CAP, D), jnp.float32)
        for block in range(N_WITHIN):
            partial_value = jnp.dot(hidden[:, block * unit_width:(block + 1) * unit_width], group_w2[group, block * unit_width:(block + 1) * unit_width], preferred_element_type=jnp.float32)
            accum_sum = accum_sum + lax.optimization_barrier(partial_value.astype(jnp.bfloat16)).astype(jnp.float32)
        result = accum_sum.astype(jnp.bfloat16)
        fetched = result[jnp.where(member, position, 0).astype(jnp.int32)]
        group_out = jnp.where(member[:, None], fetched, group_out)
    middle = residual_in + group_out.astype(jnp.float32) + group_b2[group_of]
    shared_in = layer_norm(middle, shared_gain).astype(jnp.bfloat16)
    shared_hidden = jax.nn.relu(jnp.dot(shared_in, shared_w1, preferred_element_type=jnp.float32) + shared_b1).astype(jnp.bfloat16)
    shared_out = jnp.dot(shared_hidden, shared_w2, preferred_element_type=jnp.float32)
    return (middle + shared_out + shared_b2).astype(jnp.bfloat16)
```

```python
import jax
import jax.numpy as jnp
from jax import lax
from jax.sharding import Mesh, PartitionSpec as P

X = ("xh", "xl")


def layer_norm(values, gains):
    centre = jnp.mean(values, axis=-1, keepdims=True)
    centred = values - centre
    spread = jnp.mean(centred * centred, axis=-1, keepdims=True)
    return centred * lax.rsqrt(spread + 1e-05) * gains


def shift(value, axis, step):
    size = lax.axis_size(axis)
    return lax.ppermute(value, axis, [(i, (i + step) % size) for i in range(size)])


def swap_column(value):
    return lax.ppermute(value, "xl", [(0, 1), (1, 0)])


def swap_blocks(value):
    return lax.ppermute(value, X, [(0, 3), (3, 0), (1, 2), (2, 1)])


def swap_core(value):
    return lax.ppermute(value, "core", [(0, 1), (1, 0)])


def ring_gather(rows, axis):
    half = rows.shape[0] // 2
    prev = shift(rows, axis, 1)
    foll = shift(rows, axis, -1)
    far_a = shift(prev[:half], axis, 1)
    far_b = shift(foll[half:], axis, -1)
    return rows, prev, foll, jnp.concatenate([far_a, far_b], axis=0)


def up(value):
    return value.astype(jnp.float32)


def ring_scatter(own, prev, foll, far, axis):
    half = far.shape[0] // 2
    via_prev = shift(far[:half], axis, -1)
    via_foll = shift(far[half:], axis, 1)
    prev = jnp.concatenate(
        [(up(prev[:half]) + up(via_prev)).astype(jnp.bfloat16), prev[half:]], axis=0
    )
    foll = jnp.concatenate(
        [foll[:half], (up(foll[half:]) + up(via_foll)).astype(jnp.bfloat16)], axis=0
    )
    from_foll = shift(prev, axis, -1)
    from_prev = shift(foll, axis, 1)
    return up(own) + up(from_foll) + up(from_prev)


def on_device(
    tokens,
    languages,
    lang_group,
    group_gain,
    group_w1,
    group_b1,
    group_w2,
    group_b2,
    shared_gain,
    shared_w1,
    shared_b1,
    shared_w2,
    shared_b2,
):
    tok_dev = tokens.shape[0]
    width_model = tokens.shape[1]
    num_groups = group_gain.shape[0]
    num_langs = lang_group.shape[0]
    capacity = 3 * tok_dev // (2 * num_groups)
    bf16 = jnp.bfloat16

    w1 = jnp.concatenate([group_w1[0], swap_blocks(group_w1[0])], axis=1)
    b1 = jnp.concatenate([group_b1[0], swap_blocks(group_b1[0])])
    w2 = jnp.concatenate([group_w2[0], swap_blocks(group_w2[0])], axis=0)
    sw1 = jnp.concatenate([shared_w1, swap_core(shared_w1)], axis=1)
    sb1 = jnp.concatenate([shared_b1, swap_core(shared_b1)])
    sw2 = jnp.concatenate([shared_w2, swap_core(shared_w2)], axis=0)

    residual_in = tokens.astype(jnp.float32)
    lang_hit = (languages[:, None] == jnp.arange(num_langs, dtype=jnp.int32)[None, :]).astype(
        jnp.int32
    )
    group_of = jnp.sum(lang_hit * lang_group[None, :], axis=1)
    onehot = (group_of[:, None] == jnp.arange(num_groups, dtype=jnp.int32)[None, :]).astype(
        jnp.int32
    )
    earlier = jnp.cumsum(onehot, axis=0) - onehot
    slot_index = jnp.sum(earlier * onehot, axis=1)
    position = group_of * capacity + slot_index
    dispatch_map = (
        position[None, :] == jnp.arange(num_groups * capacity, dtype=jnp.int32)[:, None]
    ).astype(bf16)
    onehot_float = onehot.astype(jnp.float32)
    row_gains = jnp.dot(onehot_float, group_gain, precision=lax.Precision.HIGHEST)
    normed = layer_norm(residual_in, row_gains).astype(bf16)
    outgoing = jnp.dot(dispatch_map, normed, preferred_element_type=jnp.float32).astype(bf16)
    outgoing = outgoing.reshape(num_groups, capacity, width_model)
    arrived = lax.all_to_all(outgoing, ("y", "core"), split_axis=0, concat_axis=0, tiled=True)
    rows = arrived.reshape(num_groups * capacity, width_model)

    cut = 7 * rows.shape[0] // 16 // 16 * 16
    part_a, part_b = rows[:cut], rows[cut:]
    size_a, size_b = part_a.shape[0], part_b.shape[0]
    pair_b = swap_column(part_b)
    a_own = jnp.concatenate(ring_gather(part_a, "z"), axis=0)
    b_all = jnp.concatenate(
        ring_gather(jnp.concatenate([part_b, pair_b], axis=0), "z"), axis=0
    )
    a_pair = swap_column(a_own)

    def feed_forward(block):
        hidden = jax.nn.relu(jnp.dot(block, w1, preferred_element_type=jnp.float32) + b1)
        return jnp.dot(hidden.astype(bf16), w2, preferred_element_type=jnp.float32)

    a_back = swap_column(feed_forward(a_pair).astype(bf16))
    b_part = feed_forward(b_all).astype(bf16)
    b_sum = ring_scatter(*jnp.split(b_part, 4), "z")
    a_part = (feed_forward(a_own) + up(a_back)).astype(bf16)
    a_sum = ring_scatter(*jnp.split(a_part, 4), "z")
    b_sum = b_sum[:size_b] + up(swap_column(b_sum[size_b:].astype(bf16)))
    summed = jnp.concatenate([a_sum, b_sum], axis=0).astype(bf16)

    returned = lax.all_to_all(
        summed.reshape(num_groups, capacity, width_model),
        ("y", "core"),
        split_axis=0,
        concat_axis=0,
        tiled=True,
    )
    returned = returned.reshape(num_groups * capacity, width_model)
    group_out = lax.dot_general(
        dispatch_map, returned, (((0,), (0,)), ((), ())), preferred_element_type=jnp.float32
    )
    group_bias = jnp.dot(onehot_float, group_b2, precision=lax.Precision.HIGHEST)
    middle = residual_in + group_out + group_bias
    shared_in = layer_norm(middle, shared_gain).astype(bf16)

    def shared_forward(block):
        hidden = jax.nn.relu(jnp.dot(block, sw1, preferred_element_type=jnp.float32) + sb1)
        return jnp.dot(hidden.astype(bf16), sw2, preferred_element_type=jnp.float32).astype(bf16)

    own, prev, foll, far = ring_gather(shared_in, "y")
    near = shared_forward(jnp.concatenate([own, prev, foll], axis=0))
    far = shared_forward(far)
    shared_out = ring_scatter(
        near[:tok_dev], near[tok_dev : 2 * tok_dev], near[2 * tok_dev :], far, "y"
    )
    return (middle + shared_out + shared_b2).astype(bf16)


def solution(mesh):
    chips = Mesh(mesh.devices.reshape(4, 2, 4, 2, 2), ("y", "core", "z", "xh", "xl"))
    group = ("y", "core")
    within = ("z", "xh", "xl")
    both = group + within
    placed = (
        P(both, None),
        P(both),
        P(),
        P(),
        P(group, None, within),
        P(group, within),
        P(group, within, None),
        P(),
        P(),
        P(None, group),
        P(group),
        P(group, None),
        P(),
    )
    return jax.shard_map(
        on_device,
        mesh=chips,
        in_specs=placed,
        out_specs=P(both, None),
        check_vma=False,
    )
```

```python
import jax
import jax.numpy as jnp
from jax import lax
from jax.sharding import Mesh, PartitionSpec as P

X = ("xh", "xl")


def layer_norm(values, gains):
    centre = jnp.mean(values, axis=-1, keepdims=True)
    centred = values - centre
    spread = jnp.mean(centred * centred, axis=-1, keepdims=True)
    return centred * lax.rsqrt(spread + 1e-05) * gains


def shift(value, axis, step):
    size = lax.axis_size(axis)
    return lax.ppermute(value, axis, [(i, (i + step) % size) for i in range(size)])


def swap_column(value):
    return lax.ppermute(value, "xl", [(0, 1), (1, 0)])


def swap_blocks(value):
    return lax.ppermute(value, X, [(0, 3), (3, 0), (1, 2), (2, 1)])


def swap_core(value):
    return lax.ppermute(value, "core", [(0, 1), (1, 0)])


def up(value):
    return value.astype(jnp.float32)


def down(value):
    return value.astype(jnp.bfloat16)


def hold(*values):
    return lax.optimization_barrier(values)


def ring_scatter(own, prev, foll, far, axis, way):
    via = up(shift(far, axis, -way))
    if way == 1:
        prev = down(up(prev) + via)
    else:
        foll = down(up(foll) + via)
    return up(own) + up(shift(prev, axis, -1)) + up(shift(foll, axis, 1))


def on_device(
    tokens,
    languages,
    lang_group,
    group_gain,
    group_w1,
    group_b1,
    group_w2,
    group_b2,
    shared_gain,
    shared_w1,
    shared_b1,
    shared_w2,
    shared_b2,
):
    tok_dev = tokens.shape[0]
    width_model = tokens.shape[1]
    num_groups = group_gain.shape[0]
    num_langs = lang_group.shape[0]
    capacity = 3 * tok_dev // (2 * num_groups)
    bf16 = jnp.bfloat16

    eighth = group_w1.shape[1] // 8
    half_model = width_model // 2
    b1_pair = swap_blocks(group_b1[0])
    w1_a, w1_b, w1_c, w1_d, w1_e = jnp.split(
        group_w1[0], [eighth, 3 * eighth, 4 * eighth, 7 * eighth]
    )
    w1_a, w1_b, w1_c = swap_blocks(w1_a), swap_blocks(w1_b), swap_blocks(w1_c)
    left, right = group_w2[0, :, :half_model], group_w2[0, :, half_model:]
    quarter = right.shape[0] // 4
    sw1_pair = swap_core(shared_w1)
    sb1_pair = swap_core(shared_b1)
    sw2_pair = swap_core(shared_w2)

    residual_in = tokens.astype(jnp.float32)
    lang_hit = (languages[:, None] == jnp.arange(num_langs, dtype=jnp.int32)[None, :]).astype(
        jnp.int32
    )
    group_of = jnp.sum(lang_hit * lang_group[None, :], axis=1)
    onehot = (group_of[:, None] == jnp.arange(num_groups, dtype=jnp.int32)[None, :]).astype(
        jnp.int32
    )
    earlier = jnp.cumsum(onehot, axis=0) - onehot
    slot_index = jnp.sum(earlier * onehot, axis=1)
    position = group_of * capacity + slot_index
    dispatch_map = (
        position[None, :] == jnp.arange(num_groups * capacity, dtype=jnp.int32)[:, None]
    ).astype(bf16)
    onehot_float = onehot.astype(jnp.float32)
    row_gains = jnp.dot(onehot_float, group_gain, precision=lax.Precision.HIGHEST)
    normed = layer_norm(residual_in, row_gains).astype(bf16)
    outgoing = jnp.dot(dispatch_map, normed, preferred_element_type=jnp.float32).astype(bf16)
    outgoing, w1_a, b1_pair, sb1_pair = hold(outgoing, w1_a, b1_pair, sb1_pair)
    outgoing = outgoing.reshape(num_groups, capacity, width_model)
    slots = capacity // 2
    count = num_groups * slots

    def exchange(value):
        return lax.all_to_all(value, ("y", "core"), split_axis=0, concat_axis=0, tiled=True)

    arrived, w1_b, sw1_pair, sw2_pair = hold(exchange(outgoing), w1_b, sw1_pair, sw2_pair)
    w1_d, _ = hold(w1_d, w1_a)
    w1_d = swap_blocks(w1_d)
    w1_e, _ = hold(w1_e, w1_b)
    w1_e = swap_blocks(w1_e)
    a_own = arrived[:, :slots].reshape(count, width_model)
    b_own = arrived[:, slots:].reshape(count, width_model)
    a_prev, a_foll = shift(a_own, "z", 1), shift(a_own, "z", -1)
    a_far = shift(a_prev, "z", 1)
    b_pair = swap_column(b_own)
    a_near = jnp.concatenate([a_own, a_prev, a_foll], axis=0)
    a_near, b_pair, w1_c = hold(a_near, b_pair, w1_c)
    (b_own,) = hold(jnp.concatenate([b_own, b_pair], axis=0))
    b_prev, b_foll = shift(b_own, "z", 1), shift(b_own, "z", -1)
    b_foll, w1_d = hold(b_foll, w1_d)
    b_far = shift(b_foll, "z", -1)
    left_out, _ = hold(left, w1_d)
    left_pair = swap_blocks(left_out)
    right_out, _ = hold(right, w1_e)
    right_a, right_b = swap_blocks(right_out[:quarter]), swap_blocks(right_out[quarter:])
    near_pair = swap_column(a_near)
    far_pair = swap_column(a_far)

    w1_pair = jnp.concatenate([w1_a, w1_b, w1_c, w1_d, w1_e], axis=0)
    w1 = jnp.concatenate([group_w1[0], w1_pair], axis=1)
    b1 = jnp.concatenate([group_b1[0], b1_pair])
    sw1 = jnp.concatenate([shared_w1, sw1_pair], axis=1)
    sb1 = jnp.concatenate([shared_b1, sb1_pair])
    sw2 = jnp.concatenate([shared_w2, sw2_pair], axis=0)
    rows = jnp.concatenate([a_near, a_far, b_own, b_foll, b_prev, near_pair, far_pair, b_far], axis=0)
    rows, w1, sw1, sw2, left_pair = hold(rows, w1, sw1, sw2, left_pair)
    hidden = down(jax.nn.relu(jnp.dot(rows, w1, preferred_element_type=jnp.float32) + b1))

    hidden, right_a = hold(hidden, right_a)
    right_pair = jnp.concatenate([right_a, right_b], axis=0)

    def second(hidden, weight, weight_pair):
        weight = jnp.concatenate([weight, weight_pair], axis=0)
        return down(jnp.dot(hidden, weight, preferred_element_type=jnp.float32))

    wide = 4 * count

    def pair_part(part):
        return part[wide + 6 * count : 2 * wide + 6 * count]

    def sums(part, a_back):
        own, foll, prev = jnp.split(part[wide : wide + 6 * count], 3)
        b_sum = ring_scatter(own, prev, foll, part[2 * wide + 6 * count :], "z", -1)
        a_part = down(up(part[:wide]) + up(a_back))
        a_sum = ring_scatter(*jnp.split(a_part, 4), "z", 1)
        b_sum = b_sum[:count] + up(swap_column(down(b_sum[count:])))
        shape = (num_groups, slots, part.shape[1])
        summed = jnp.concatenate([a_sum.reshape(shape), b_sum.reshape(shape)], axis=1)
        return exchange(down(summed))

    part_l = second(hidden, left, left_pair)
    back_l = swap_column(pair_part(part_l))
    hidden, back_l = hold(hidden, back_l)
    part_r = second(hidden, right, right_pair)
    back_r = swap_column(pair_part(part_r))
    returned = jnp.concatenate([sums(part_l, back_l), sums(part_r, back_r)], axis=2)
    returned = returned.reshape(num_groups * capacity, width_model)
    group_out = lax.dot_general(
        dispatch_map, returned, (((0,), (0,)), ((), ())), preferred_element_type=jnp.float32
    )
    group_bias = jnp.dot(onehot_float, group_b2, precision=lax.Precision.HIGHEST)
    middle = residual_in + group_out + group_bias
    shared_in = layer_norm(middle, shared_gain).astype(bf16)

    def shared_forward(block):
        hidden = jax.nn.relu(jnp.dot(block, sw1, preferred_element_type=jnp.float32) + sb1)
        return jnp.dot(hidden.astype(bf16), sw2, preferred_element_type=jnp.float32).astype(bf16)

    def shared_sums(own, way):
        prev, foll = shift(own, "y", 1), shift(own, "y", -1)
        far = shift(prev if way == 1 else foll, "y", way)
        part = shared_forward(jnp.concatenate([own, prev, foll, far], axis=0))
        return ring_scatter(*jnp.split(part, 4), "y", way)

    half_tok = tok_dev // 2
    shared_out = jnp.concatenate(
        [shared_sums(shared_in[:half_tok], 1), shared_sums(shared_in[half_tok:], -1)], axis=0
    )
    return (middle + shared_out + shared_b2).astype(bf16)


def solution(mesh):
    chips = Mesh(mesh.devices.reshape(4, 2, 4, 2, 2), ("y", "core", "z", "xh", "xl"))
    group = ("y", "core")
    within = ("z", "xh", "xl")
    both = group + within
    placed = (
        P(both, None),
        P(both),
        P(),
        P(),
        P(group, None, within),
        P(group, within),
        P(group, within, None),
        P(),
        P(),
        P(None, group),
        P(group),
        P(group, None),
        P(),
    )
    return jax.shard_map(
        on_device,
        mesh=chips,
        in_specs=placed,
        out_specs=P(both, None),
        check_vma=False,
    )
```

```python
import jax
import jax.numpy as jnp
from jax import lax
from jax.sharding import Mesh, PartitionSpec as P

X = ("xh", "xl")


def layer_norm(values, gains):
    centre = jnp.mean(values, axis=-1, keepdims=True)
    centred = values - centre
    spread = jnp.mean(centred * centred, axis=-1, keepdims=True)
    return centred * lax.rsqrt(spread + 1e-05) * gains


def shift(value, axis, step):
    size = lax.axis_size(axis)
    return lax.ppermute(value, axis, [(i, (i + step) % size) for i in range(size)])


def swap_column(value):
    return lax.ppermute(value, "xl", [(0, 1), (1, 0)])


def swap_blocks(value):
    return lax.ppermute(value, X, [(0, 3), (3, 0), (1, 2), (2, 1)])


def swap_core(value):
    return lax.ppermute(value, "core", [(0, 1), (1, 0)])


def up(value):
    return value.astype(jnp.float32)


def down(value):
    return value.astype(jnp.bfloat16)


def hold(*values):
    return lax.optimization_barrier(values)


def ring_scatter(own, prev, foll, far, axis, way):
    via = up(shift(far, axis, -way))
    if way == 1:
        prev = down(up(prev) + via)
    else:
        foll = down(up(foll) + via)
    return up(own) + up(shift(prev, axis, -1)) + up(shift(foll, axis, 1))


def on_device(
    tokens,
    languages,
    lang_group,
    group_gain,
    group_w1,
    group_b1,
    group_w2,
    group_b2,
    shared_gain,
    shared_w1,
    shared_b1,
    shared_w2,
    shared_b2,
):
    tok_dev = tokens.shape[0]
    width_model = tokens.shape[1]
    num_groups = group_gain.shape[0]
    num_langs = lang_group.shape[0]
    capacity = 3 * tok_dev // (2 * num_groups)
    bf16 = jnp.bfloat16

    half_model = width_model // 2
    b1_pair = swap_blocks(group_b1[0])
    w1_pair = swap_blocks(group_w1[0])
    left, right = group_w2[0, :, :half_model], group_w2[0, :, half_model:]
    sw1_pair = swap_core(shared_w1)
    sb1_pair = swap_core(shared_b1)
    sw2_pair = swap_core(shared_w2)

    residual_in = tokens.astype(jnp.float32)
    lang_hit = (languages[:, None] == jnp.arange(num_langs, dtype=jnp.int32)[None, :]).astype(
        jnp.int32
    )
    group_of = jnp.sum(lang_hit * lang_group[None, :], axis=1)
    onehot = (group_of[:, None] == jnp.arange(num_groups, dtype=jnp.int32)[None, :]).astype(
        jnp.int32
    )
    earlier = jnp.cumsum(onehot, axis=0) - onehot
    slot_index = jnp.sum(earlier * onehot, axis=1)
    position = group_of * capacity + slot_index
    dispatch_map = (
        position[None, :] == jnp.arange(num_groups * capacity, dtype=jnp.int32)[:, None]
    ).astype(bf16)
    onehot_float = onehot.astype(jnp.float32)
    row_gains = jnp.dot(onehot_float, group_gain, precision=lax.Precision.HIGHEST)
    normed = layer_norm(residual_in, row_gains).astype(bf16)
    outgoing = jnp.dot(dispatch_map, normed, preferred_element_type=jnp.float32).astype(bf16)
    outgoing = outgoing.reshape(num_groups, capacity, width_model)
    slots = capacity // 2
    count = num_groups * slots

    def exchange(value):
        return lax.all_to_all(value, ("y", "core"), split_axis=0, concat_axis=0, tiled=True)

    arrived, sw1_pair, sw2_pair, sb1_pair = hold(exchange(outgoing), sw1_pair, sw2_pair, sb1_pair)
    a_own = arrived[:, :slots].reshape(count, width_model)
    b_own = arrived[:, slots:].reshape(count, width_model)
    a_prev, a_foll = shift(a_own, "z", 1), shift(a_own, "z", -1)
    a_far = shift(a_prev, "z", 1)
    b_pair = swap_column(b_own)
    a_near = jnp.concatenate([a_own, a_prev, a_foll], axis=0)
    a_near, b_pair = hold(a_near, b_pair)
    (b_own,) = hold(jnp.concatenate([b_own, b_pair], axis=0))
    b_prev, b_foll = shift(b_own, "z", 1), shift(b_own, "z", -1)
    b_far = shift(b_foll, "z", -1)
    near_pair = swap_column(a_near)
    far_own, w1_pair = hold(a_far, w1_pair)
    far_pair = swap_column(far_own)
    left_out, _ = hold(left, w1_pair)
    left_pair = swap_blocks(left_out)
    right_out, _ = hold(right, w1_pair, b_foll)[:2]
    right_pair = swap_blocks(right_out)
    w1 = jnp.concatenate([group_w1[0], w1_pair], axis=1)
    b1 = jnp.concatenate([group_b1[0], b1_pair])
    rows = jnp.concatenate([a_near, a_far, b_own, b_foll, b_prev, near_pair, far_pair, b_far], axis=0)
    rows, w1, left_pair = hold(rows, w1, left_pair)
    hidden = down(jax.nn.relu(jnp.dot(rows, w1, preferred_element_type=jnp.float32) + b1))

    def second(hidden, weight, weight_pair):
        weight = jnp.concatenate([weight, weight_pair], axis=0)
        return down(jnp.dot(hidden, weight, preferred_element_type=jnp.float32))

    wide = 4 * count

    def pair_part(part):
        return part[wide + 6 * count : 2 * wide + 6 * count]

    def sums(weight, weight_pair, hidden, after):
        part = second(hidden, weight, weight_pair)
        a_back = swap_column(pair_part(part))
        own, foll, prev = jnp.split(part[wide : wide + 6 * count], 3)
        foll = down(up(foll) + up(shift(part[2 * wide + 6 * count :], "z", 1)))
        b_sum = up(own) + up(shift(prev, "z", -1)) + up(shift(foll, "z", 1))
        a_back, after = hold(a_back, after)
        a_part = down(up(part[:wide]) + up(a_back))
        own, prev, foll, far = jnp.split(a_part, 4)
        far = shift(far, "z", -1)
        b_back = swap_column(down(b_sum[count:]))
        hidden, far, b_back = hold(hidden, far, b_back)
        prev = down(up(prev) + up(far))
        a_sum = up(own) + up(shift(prev, "z", -1)) + up(shift(foll, "z", 1))
        b_sum = b_sum[:count] + up(b_back)
        shape = (num_groups, slots, part.shape[1])
        summed = jnp.concatenate([a_sum.reshape(shape), b_sum.reshape(shape)], axis=1)
        return exchange(down(summed)), hidden, after

    return_l, hidden, right_pair = sums(left, left_pair, hidden, right_pair)
    return_r, _, _ = sums(right, right_pair, hidden, b1)
    returned = jnp.concatenate([return_l, return_r], axis=2)
    returned = returned.reshape(num_groups * capacity, width_model)
    group_out = lax.dot_general(
        dispatch_map, returned, (((0,), (0,)), ((), ())), preferred_element_type=jnp.float32
    )
    group_bias = jnp.dot(onehot_float, group_b2, precision=lax.Precision.HIGHEST)
    middle = residual_in + group_out + group_bias
    shared_in = layer_norm(middle, shared_gain).astype(bf16)

    def shared_forward(block):
        hidden = [
            down(jax.nn.relu(jnp.dot(block, w, preferred_element_type=jnp.float32) + b))
            for w, b in ((shared_w1, shared_b1), (sw1_pair, sb1_pair))
        ]
        hidden = hold(*hidden)
        return down(
            jnp.dot(hidden[0], shared_w2, preferred_element_type=jnp.float32)
            + jnp.dot(hidden[1], sw2_pair, preferred_element_type=jnp.float32)
        )

    def shared_sums(own, way):
        prev, foll = shift(own, "y", 1), shift(own, "y", -1)
        far = shift(prev if way == 1 else foll, "y", way)
        part = shared_forward(jnp.concatenate([own, prev, foll, far], axis=0))
        return ring_scatter(*jnp.split(part, 4), "y", way)

    half_tok = tok_dev // 2
    shared_out = jnp.concatenate(
        [shared_sums(shared_in[:half_tok], 1), shared_sums(shared_in[half_tok:], -1)], axis=0
    )
    return (middle + shared_out + shared_b2).astype(bf16)


def solution(mesh):
    chips = Mesh(mesh.devices.reshape(4, 2, 4, 2, 2), ("y", "core", "z", "xh", "xl"))
    group = ("y", "core")
    within = ("z", "xh", "xl")
    both = group + within
    placed = (
        P(both, None),
        P(both),
        P(),
        P(),
        P(group, None, within),
        P(group, within),
        P(group, within, None),
        P(),
        P(),
        P(None, group),
        P(group),
        P(group, None),
        P(),
    )
    return jax.shard_map(
        on_device,
        mesh=chips,
        in_specs=placed,
        out_specs=P(both, None),
        check_vma=False,
    )
```

```python
import jax
import jax.numpy as jnp
from jax import lax
from jax.sharding import Mesh, PartitionSpec as P

X = ("xh", "xl")


def layer_norm(values, gains):
    centre = jnp.mean(values, axis=-1, keepdims=True)
    centred = values - centre
    spread = jnp.mean(centred * centred, axis=-1, keepdims=True)
    return centred * lax.rsqrt(spread + 1e-05) * gains


def shift(value, axis, step):
    size = lax.axis_size(axis)
    return lax.ppermute(value, axis, [(i, (i + step) % size) for i in range(size)])


def swap_column(value):
    return lax.ppermute(value, "xl", [(0, 1), (1, 0)])


def swap_blocks(value):
    return lax.ppermute(value, X, [(0, 3), (3, 0), (1, 2), (2, 1)])


def swap_core(value):
    return lax.ppermute(value, "core", [(0, 1), (1, 0)])


def up(value):
    return value.astype(jnp.float32)


def down(value):
    return value.astype(jnp.bfloat16)


def hold(*values):
    return lax.optimization_barrier(values)


def ring_scatter(own, prev, foll, far, axis, way):
    via = up(shift(far, axis, -way))
    if way == 1:
        prev = down(up(prev) + via)
    else:
        foll = down(up(foll) + via)
    return up(own) + up(shift(prev, axis, -1)) + up(shift(foll, axis, 1))


def on_device(
    tokens,
    languages,
    lang_group,
    group_gain,
    group_w1,
    group_b1,
    group_w2,
    group_b2,
    shared_gain,
    shared_w1,
    shared_b1,
    shared_w2,
    shared_b2,
):
    tok_dev = tokens.shape[0]
    width_model = tokens.shape[1]
    num_groups = group_gain.shape[0]
    num_langs = lang_group.shape[0]
    capacity = 3 * tok_dev // (2 * num_groups)
    bf16 = jnp.bfloat16

    half_model = width_model // 2
    b1_pair = swap_blocks(group_b1[0])
    w1_out, b1_pair = hold(group_w1[0], b1_pair)
    w1_pair = swap_blocks(w1_out)
    left, right = group_w2[0, :, :half_model], group_w2[0, :, half_model:]
    sw1_pair = swap_core(shared_w1)
    sb1_pair = swap_core(shared_b1)
    sw2_pair = swap_core(shared_w2)

    residual_in = tokens.astype(jnp.float32)
    lang_hit = (languages[:, None] == jnp.arange(num_langs, dtype=jnp.int32)[None, :]).astype(
        jnp.int32
    )
    group_of = jnp.sum(lang_hit * lang_group[None, :], axis=1)
    onehot = (group_of[:, None] == jnp.arange(num_groups, dtype=jnp.int32)[None, :]).astype(
        jnp.int32
    )
    earlier = jnp.cumsum(onehot, axis=0) - onehot
    slot_index = jnp.sum(earlier * onehot, axis=1)
    position = group_of * capacity + slot_index
    dispatch_map = (
        position[None, :] == jnp.arange(num_groups * capacity, dtype=jnp.int32)[:, None]
    ).astype(bf16)
    onehot_float = onehot.astype(jnp.float32)
    row_gains = jnp.dot(onehot_float, group_gain, precision=lax.Precision.HIGHEST)
    normed = layer_norm(residual_in, row_gains).astype(bf16)
    outgoing = jnp.dot(dispatch_map, normed, preferred_element_type=jnp.float32).astype(bf16)
    outgoing = outgoing.reshape(num_groups, capacity, width_model)
    slots = capacity // 2
    count = num_groups * slots

    def exchange(value):
        return lax.all_to_all(value, ("y", "core"), split_axis=0, concat_axis=0, tiled=True)

    arrived, sw1_pair, sw2_pair, sb1_pair = hold(exchange(outgoing), sw1_pair, sw2_pair, sb1_pair)
    a_own = arrived[:, :slots].reshape(count, width_model)
    b_own = arrived[:, slots:].reshape(count, width_model)
    a_prev, a_foll = shift(a_own, "z", 1), shift(a_own, "z", -1)
    a_far = shift(a_prev, "z", 1)
    b_pair = swap_column(b_own)
    a_near = jnp.concatenate([a_own, a_prev, a_foll], axis=0)
    a_near, b_pair = hold(a_near, b_pair)
    (b_own,) = hold(jnp.concatenate([b_own, b_pair], axis=0))
    b_prev, b_foll = shift(b_own, "z", 1), shift(b_own, "z", -1)
    b_far = shift(b_foll, "z", -1)
    near_pair = swap_column(a_near)
    far_own, w1_pair = hold(a_far, w1_pair)
    far_pair = swap_column(far_own)
    left_out, _ = hold(left, w1_pair)
    left_pair = swap_blocks(left_out)
    right_out, _ = hold(right, w1_pair, b_foll)[:2]
    right_pair = swap_blocks(right_out)
    w1 = jnp.concatenate([group_w1[0], w1_pair], axis=1)
    b1 = jnp.concatenate([group_b1[0], b1_pair])
    rows = jnp.concatenate([a_near, a_far, b_own, b_foll, b_prev, near_pair, far_pair, b_far], axis=0)
    rows, w1, left_pair = hold(rows, w1, left_pair)
    hidden = down(jax.nn.relu(jnp.dot(rows, w1, preferred_element_type=jnp.float32) + b1))

    def second(hidden, weight, weight_pair):
        weight = jnp.concatenate([weight, weight_pair], axis=0)
        return down(jnp.dot(hidden, weight, preferred_element_type=jnp.float32))

    def block(part, step):
        at = {"own": (0, 4, 10, 5), "prev": (1, 8, 11, 9), "foll": (2, 6, 12, 7), "far": (3, 14, 13, 15)}
        return jnp.concatenate([part[i * count : (i + 1) * count] for i in at[step]], axis=0)

    def sums(weight, weight_pair, hidden, after, way):
        part = second(hidden, weight, weight_pair)
        own, prev, foll = (block(part, step) for step in ("own", "prev", "foll"))
        via = shift(block(part, "far"), "z", -way)
        if way == 1:
            foll = shift(foll, "z", 1)
            via, foll, after = hold(via, foll, after)
            prev = down(up(prev) + up(via))
            hidden, prev = hold(hidden, prev)
            prev = shift(prev, "z", -1)
        else:
            prev = shift(prev, "z", -1)
            via, prev, after = hold(via, prev, after)
            foll = down(up(foll) + up(via))
            foll = shift(foll, "z", 1)
        summed = up(own) + up(prev) + up(foll)
        outer = down(summed[2 * count :])
        summed = summed[: 2 * count] + up(swap_column(outer))
        summed = down(summed).reshape(2, num_groups, slots, part.shape[1])
        return exchange(jnp.concatenate([summed[0], summed[1]], axis=1)), hidden, after, outer

    return_l, hidden, right_pair, outer = sums(left, left_pair, hidden, right_pair, 1)
    return_r, _, _, _ = sums(right, right_pair, hidden, outer, -1)
    returned = jnp.concatenate([return_l, return_r], axis=2)
    returned = returned.reshape(num_groups * capacity, width_model)
    group_out = lax.dot_general(
        dispatch_map, returned, (((0,), (0,)), ((), ())), preferred_element_type=jnp.float32
    )
    group_bias = jnp.dot(onehot_float, group_b2, precision=lax.Precision.HIGHEST)
    middle = residual_in + group_out + group_bias
    shared_in = layer_norm(middle, shared_gain).astype(bf16)

    def shared_forward(block):
        hidden = [
            down(jax.nn.relu(jnp.dot(block, w, preferred_element_type=jnp.float32) + b))
            for w, b in ((shared_w1, shared_b1), (sw1_pair, sb1_pair))
        ]
        hidden = hold(*hidden)
        return down(
            jnp.dot(hidden[0], shared_w2, preferred_element_type=jnp.float32)
            + jnp.dot(hidden[1], sw2_pair, preferred_element_type=jnp.float32)
        )

    def shared_gather(own, way):
        prev, foll = shift(own, "y", 1), shift(own, "y", -1)
        far = shift(prev if way == 1 else foll, "y", way)
        return jnp.concatenate([own, prev, foll, far], axis=0), (prev, foll)

    half_tok = tok_dev // 2
    first, near = shared_gather(shared_in[:half_tok], 1)
    second_in, near = hold(shared_in[half_tok:], near)
    other, _ = shared_gather(second_in, -1)
    first = ring_scatter(*jnp.split(shared_forward(first), 4), "y", 1)
    other = ring_scatter(*jnp.split(shared_forward(other), 4), "y", -1)
    shared_out = jnp.concatenate([first, other], axis=0)
    return (middle + shared_out + shared_b2).astype(bf16)


def solution(mesh):
    chips = Mesh(mesh.devices.reshape(4, 2, 4, 2, 2), ("y", "core", "z", "xh", "xl"))
    group = ("y", "core")
    within = ("z", "xh", "xl")
    both = group + within
    placed = (
        P(both, None),
        P(both),
        P(),
        P(),
        P(group, None, within),
        P(group, within),
        P(group, within, None),
        P(),
        P(),
        P(None, group),
        P(group),
        P(group, None),
        P(),
    )
    return jax.shard_map(
        on_device,
        mesh=chips,
        in_specs=placed,
        out_specs=P(both, None),
        check_vma=False,
    )
```

```python
import jax
import jax.numpy as jnp
from jax import lax
from jax.sharding import Mesh, PartitionSpec as P

X = ("xh", "xl")


def layer_norm(values, gains):
    centre = jnp.mean(values, axis=-1, keepdims=True)
    centred = values - centre
    spread = jnp.mean(centred * centred, axis=-1, keepdims=True)
    return centred * lax.rsqrt(spread + 1e-05) * gains


def shift(value, axis, step):
    size = lax.axis_size(axis)
    return lax.ppermute(value, axis, [(i, (i + step) % size) for i in range(size)])


def swap_column(value):
    return lax.ppermute(value, "xl", [(0, 1), (1, 0)])


def swap_blocks(value):
    return lax.ppermute(value, X, [(0, 3), (3, 0), (1, 2), (2, 1)])


def swap_core(value):
    return lax.ppermute(value, "core", [(0, 1), (1, 0)])


def up(value):
    return value.astype(jnp.float32)


def down(value):
    return value.astype(jnp.bfloat16)


def hold(*values):
    return lax.optimization_barrier(values)


def ring_scatter(own, prev, foll, far, axis, way):
    via = up(shift(far, axis, -way))
    if way == 1:
        prev = down(up(prev) + via)
    else:
        foll = down(up(foll) + via)
    return up(own) + up(shift(prev, axis, -1)) + up(shift(foll, axis, 1))


def pick(index, table):
    rows = jnp.broadcast_to(table[0], (index.shape[0], table.shape[1]))
    for i in range(1, table.shape[0]):
        rows = jnp.where((index == i)[:, None], table[i], rows)
    return rows


def on_device(
    tokens,
    languages,
    lang_group,
    group_gain,
    group_w1,
    group_b1,
    group_w2,
    group_b2,
    shared_gain,
    shared_w1,
    shared_b1,
    shared_w2,
    shared_b2,
):
    tok_dev = tokens.shape[0]
    width_model = tokens.shape[1]
    num_groups = group_gain.shape[0]
    num_langs = lang_group.shape[0]
    capacity = 3 * tok_dev // (2 * num_groups)
    bf16 = jnp.bfloat16

    half_model = width_model // 2
    left, right = group_w2[0, :, :half_model], group_w2[0, :, half_model:]
    rest, parts = group_b1[0], []
    for _ in range(3):
        parts.append(lax.reduce_precision(rest, 8, 7))
        rest = rest - parts[-1]
    parts = down(jnp.stack(parts + [jnp.zeros_like(rest)] * 5))
    w1_pair = swap_blocks(jnp.concatenate([group_w1[0], parts], axis=0))

    residual_in = tokens.astype(jnp.float32)
    lang_hit = (languages[:, None] == jnp.arange(num_langs, dtype=jnp.int32)[None, :]).astype(
        jnp.int32
    )
    group_of = jnp.sum(lang_hit * lang_group[None, :], axis=1)
    onehot = (group_of[:, None] == jnp.arange(num_groups, dtype=jnp.int32)[None, :]).astype(
        jnp.int32
    )
    earlier = jnp.cumsum(onehot, axis=0) - onehot
    slot_index = jnp.sum(earlier * onehot, axis=1)
    position = group_of * capacity + slot_index
    dispatch_map = (
        position[None, :] == jnp.arange(num_groups * capacity, dtype=jnp.int32)[:, None]
    ).astype(bf16)
    row_gains = pick(group_of, group_gain)
    normed = layer_norm(residual_in, row_gains).astype(bf16)
    outgoing = jnp.dot(dispatch_map, normed, preferred_element_type=jnp.float32).astype(bf16)
    count = num_groups * capacity // 2

    def exchange(value):
        value = value.reshape(num_groups, capacity, value.shape[-1])
        value = lax.all_to_all(value, ("y", "core"), split_axis=0, concat_axis=0, tiled=True)
        return value.reshape(2 * count, value.shape[-1])

    arrived, sw1_pair, sw2_pair, sb1_pair = hold(
        exchange(outgoing), swap_core(shared_w1), swap_core(shared_w2), swap_core(shared_b1)
    )
    a_own, b_own = arrived[:count], arrived[count:]
    a_prev, a_foll = shift(a_own, "z", 1), shift(a_own, "z", -1)
    a_far = shift(a_prev, "z", 1)
    b_pair = swap_column(b_own)
    a_near = jnp.concatenate([a_own, a_prev, a_foll], axis=0)
    a_near, b_pair = hold(a_near, b_pair)
    (b_own,) = hold(jnp.concatenate([b_own, b_pair], axis=0))
    b_prev, b_foll = shift(b_own, "z", 1), shift(b_own, "z", -1)
    b_foll, w1_pair = hold(b_foll, w1_pair)
    b_far = shift(b_foll, "z", -1)
    near_pair = swap_column(a_near)
    far_pair = swap_column(a_far)
    left_out, _ = hold(left, a_far)
    left_pair = swap_blocks(left_out)
    right_out, _, _ = hold(right, w1_pair, b_prev)
    right_pair = swap_blocks(right_out)
    b1_pair = jnp.sum(up(w1_pair[width_model:]), axis=0)
    w1 = jnp.concatenate([group_w1[0], w1_pair[:width_model]], axis=1)
    b1 = jnp.concatenate([group_b1[0], b1_pair])
    rows = jnp.concatenate([a_near, a_far, b_own, b_foll, b_prev, near_pair, far_pair, b_far], axis=0)
    hidden = down(jax.nn.relu(jnp.dot(rows, w1, preferred_element_type=jnp.float32) + b1))

    def second(hidden, weight, weight_pair):
        weight = jnp.concatenate([weight, weight_pair], axis=0)
        return down(jnp.dot(hidden, weight, preferred_element_type=jnp.float32))

    def block(part, step):
        at = {"own": (0, 4, 10, 5), "prev": (1, 8, 11, 9), "foll": (2, 6, 12, 7), "far": (3, 14, 13, 15)}
        return jnp.concatenate([part[i * count : (i + 1) * count] for i in at[step]], axis=0)

    def ring(weight, weight_pair, hidden, way, after):
        part = second(hidden, weight, weight_pair)
        own, prev, foll = (block(part, step) for step in ("own", "prev", "foll"))
        via = shift(block(part, "far"), "z", -way)
        if way == 1:
            foll = shift(foll, "z", 1)
            via, foll, after = hold(via, foll, after)
            prev = down(up(prev) + up(via))
            hidden, prev = hold(hidden, prev)
            prev = shift(prev, "z", -1)
        else:
            prev = shift(prev, "z", -1)
            via, after = hold(via, after)
            foll = shift(down(up(foll) + up(via)), "z", 1)
        return up(own) + up(prev) + up(foll), hidden, after

    def finish(summed, back):
        return exchange(down(summed[: 2 * count] + up(back)))

    sum_l, hidden, right_pair = ring(left, left_pair, hidden, 1, right_pair)
    out_l = down(sum_l[2 * count :])
    back_l = swap_column(out_l)
    sum_r, _, back_l = ring(right, right_pair, hidden, -1, back_l)
    return_l = finish(sum_l, back_l)
    back_r = swap_column(down(sum_r[2 * count :]))
    return_r = finish(sum_r, back_r)
    returned = jnp.concatenate([return_l, return_r], axis=1)
    group_out = lax.dot_general(
        dispatch_map, returned, (((0,), (0,)), ((), ())), preferred_element_type=jnp.float32
    )
    group_bias = pick(group_of, group_b2)
    middle = residual_in + group_out + group_bias
    shared_in = layer_norm(middle, shared_gain).astype(bf16)

    def shared_forward(block):
        hidden = [
            down(jax.nn.relu(jnp.dot(block, w, preferred_element_type=jnp.float32) + b))
            for w, b in ((shared_w1, shared_b1), (sw1_pair, sb1_pair))
        ]
        hidden = hold(*hidden)
        return down(
            jnp.dot(hidden[0], shared_w2, preferred_element_type=jnp.float32)
            + jnp.dot(hidden[1], sw2_pair, preferred_element_type=jnp.float32)
        )

    half_tok = tok_dev // 2
    one, two = shared_in[:half_tok], shared_in[half_tok:]
    prev, foll = shift(one, "y", 1), shift(one, "y", -1)
    far = shift(prev, "y", 1)
    first = jnp.concatenate([one, prev, foll, far], axis=0)
    held, _, _ = hold(two, prev, foll)
    foll = shift(held, "y", -1)
    held, _ = hold(two, far)
    prev = shift(held, "y", 1)
    far = shift(foll, "y", -1)
    other = jnp.concatenate([two, prev, foll, far], axis=0)
    first = ring_scatter(*jnp.split(shared_forward(first), 4), "y", 1)
    other = ring_scatter(*jnp.split(shared_forward(other), 4), "y", -1)
    shared_out = jnp.concatenate([first, other], axis=0)
    return (middle + shared_out + shared_b2).astype(bf16)


def solution(mesh):
    chips = Mesh(mesh.devices.reshape(4, 2, 4, 2, 2), ("y", "core", "z", "xh", "xl"))
    group = ("y", "core")
    within = ("z", "xh", "xl")
    both = group + within
    placed = (
        P(both, None),
        P(both),
        P(),
        P(),
        P(group, None, within),
        P(group, within),
        P(group, within, None),
        P(),
        P(),
        P(None, group),
        P(group),
        P(group, None),
        P(),
    )
    return jax.shard_map(
        on_device,
        mesh=chips,
        in_specs=placed,
        out_specs=P(both, None),
        check_vma=False,
    )
```

```python
import jax
import jax.numpy as jnp
from jax import lax
from jax.experimental import pallas as pl
from jax.experimental.pallas import tpu as pltpu
from jax.sharding import Mesh, PartitionSpec as P

X = ("xh", "xl")


def layer_norm(values, gains):
    centre = jnp.mean(values, axis=-1, keepdims=True)
    centred = values - centre
    spread = jnp.mean(centred * centred, axis=-1, keepdims=True)
    return centred * lax.rsqrt(spread + 1e-05) * gains


def shift(value, axis, step):
    size = lax.axis_size(axis)
    return lax.ppermute(value, axis, [(i, (i + step) % size) for i in range(size)])


def swap_column(value):
    return lax.ppermute(value, "xl", [(0, 1), (1, 0)])


def swap_blocks(value):
    return lax.ppermute(value, X, [(0, 3), (3, 0), (1, 2), (2, 1)])


def swap_core(value):
    return lax.ppermute(value, "core", [(0, 1), (1, 0)])


def up(value):
    return value.astype(jnp.float32)


def down(value):
    return value.astype(jnp.bfloat16)


def hold(*values):
    return lax.optimization_barrier(values)


def ring_scatter(own, prev, foll, far, axis, way):
    via = up(shift(far, axis, -way))
    if way == 1:
        prev = down(up(prev) + via)
    else:
        foll = down(up(foll) + via)
    return up(own) + up(shift(prev, axis, -1)) + up(shift(foll, axis, 1))


def on_chip(value):
    def copy(source, target):
        pltpu.sync_copy(source, target)

    return pl.pallas_call(
        copy,
        in_specs=[pl.BlockSpec(memory_space=pl.ANY)],
        out_specs=pl.BlockSpec(memory_space=pltpu.VMEM),
        out_shape=pltpu.VMEM(value.shape, value.dtype),
        compiler_params=pltpu.CompilerParams(vmem_limit_bytes=262144),
        name="on_chip",
    )(value)


def pick(index, table):
    rows = jnp.broadcast_to(table[0], (index.shape[0], table.shape[1]))
    for i in range(1, table.shape[0]):
        rows = jnp.where((index == i)[:, None], table[i], rows)
    return rows


def on_device(
    tokens,
    languages,
    lang_group,
    group_gain,
    group_w1,
    group_b1,
    group_w2,
    group_b2,
    shared_gain,
    shared_w1,
    shared_b1,
    shared_w2,
    shared_b2,
):
    tok_dev = tokens.shape[0]
    width_model = tokens.shape[1]
    num_groups = group_gain.shape[0]
    num_langs = lang_group.shape[0]
    capacity = 3 * tok_dev // (2 * num_groups)
    bf16 = jnp.bfloat16

    half_model = width_model // 2
    left, right = group_w2[0, :, :half_model], group_w2[0, :, half_model:]
    w1_out, b1_pair = hold(group_w1[0], swap_blocks(group_b1[0]))
    w1_pair = swap_blocks(w1_out)

    residual_in = tokens.astype(jnp.float32)
    lang_hit = (languages[:, None] == jnp.arange(num_langs, dtype=jnp.int32)[None, :]).astype(
        jnp.int32
    )
    group_of = jnp.sum(lang_hit * lang_group[None, :], axis=1)
    onehot = (group_of[:, None] == jnp.arange(num_groups, dtype=jnp.int32)[None, :]).astype(
        jnp.int32
    )
    earlier = jnp.cumsum(onehot, axis=0) - onehot
    slot_index = jnp.sum(earlier * onehot, axis=1)
    position = group_of * capacity + slot_index
    dispatch_map = (
        position[None, :] == jnp.arange(num_groups * capacity, dtype=jnp.int32)[:, None]
    ).astype(bf16)
    row_gains = pick(group_of, group_gain)
    normed = layer_norm(residual_in, row_gains).astype(bf16)
    outgoing = jnp.dot(dispatch_map, normed, preferred_element_type=jnp.float32).astype(bf16)
    count = num_groups * capacity // 2

    def exchange(value):
        value = value.reshape(num_groups, capacity, value.shape[-1])
        value = lax.all_to_all(value, ("y", "core"), split_axis=0, concat_axis=0, tiled=True)
        return value.reshape(2 * count, value.shape[-1])

    arrived, sw1_pair, sw2_pair, sb1_pair = hold(
        exchange(outgoing), swap_core(shared_w1), swap_core(shared_w2), swap_core(shared_b1)
    )
    a_own, b_own = arrived[:count], arrived[count:]
    a_prev, a_foll = shift(a_own, "z", 1), shift(a_own, "z", -1)
    a_far = shift(a_prev, "z", 1)
    b_pair = swap_column(b_own)
    a_near = jnp.concatenate([a_own, a_prev, a_foll], axis=0)
    a_near, b_pair = hold(a_near, b_pair)
    (b_own,) = hold(jnp.concatenate([b_own, b_pair], axis=0))
    b_foll = shift(b_own, "z", -1)
    held, a_far = hold(b_own, a_far)
    b_prev = shift(held, "z", 1)
    sw1_pair, sw2_pair, _ = hold(sw1_pair, sw2_pair, b_own)
    sw1_pair, sw2_pair = on_chip(sw1_pair), on_chip(sw2_pair)
    b_foll, w1_pair, sw1_pair, sw2_pair = hold(b_foll, w1_pair, sw1_pair, sw2_pair)
    b_far = shift(b_foll, "z", -1)
    near_pair = swap_column(a_near)
    far_pair = swap_column(a_far)
    left_out, _ = hold(left, a_far)
    left_pair = swap_blocks(left_out)
    right_out, _, _ = hold(right, w1_pair, b_prev)
    right_pair = swap_blocks(right_out)
    w1 = jnp.concatenate([group_w1[0], w1_pair], axis=1)
    b1 = jnp.concatenate([group_b1[0], b1_pair])
    rows = jnp.concatenate([a_near, a_far, b_own, b_foll, b_prev, near_pair, far_pair, b_far], axis=0)
    hidden = down(jax.nn.relu(jnp.dot(rows, w1, preferred_element_type=jnp.float32) + b1))

    def second(hidden, weight, weight_pair):
        weight = jnp.concatenate([weight, weight_pair], axis=0)
        return down(jnp.dot(hidden, weight, preferred_element_type=jnp.float32))

    def block(part, step):
        at = {"own": (0, 4, 10, 5), "prev": (1, 8, 11, 9), "foll": (2, 6, 12, 7), "far": (3, 14, 13, 15)}
        return jnp.concatenate([part[i * count : (i + 1) * count] for i in at[step]], axis=0)

    def ring(weight, weight_pair, hidden, way, after):
        part = second(hidden, weight, weight_pair)
        own, prev, foll = (block(part, step) for step in ("own", "prev", "foll"))
        via = shift(block(part, "far"), "z", -way)
        if way == 1:
            foll = shift(foll, "z", 1)
            via, foll, after = hold(via, foll, after)
            prev = down(up(prev) + up(via))
            hidden, prev = hold(hidden, prev)
            prev = shift(prev, "z", -1)
        else:
            prev = shift(prev, "z", -1)
            via, after = hold(via, after)
            foll = shift(down(up(foll) + up(via)), "z", 1)
        return up(own) + up(prev) + up(foll), hidden, after

    def finish(summed, back):
        return exchange(down(summed[: 2 * count] + up(back)))

    sum_l, hidden, right_pair = ring(left, left_pair, hidden, 1, right_pair)
    out_l = down(sum_l[2 * count :])
    back_l = swap_column(out_l)
    sum_r, _, back_l = ring(right, right_pair, hidden, -1, back_l)
    return_l = finish(sum_l, back_l)
    sum_r, return_l = hold(sum_r, return_l)
    back_r = swap_column(down(sum_r[2 * count :]))
    return_r = finish(sum_r, back_r)
    returned = jnp.concatenate([return_l, return_r], axis=1)
    group_out = lax.dot_general(
        dispatch_map, returned, (((0,), (0,)), ((), ())), preferred_element_type=jnp.float32
    )
    group_bias = pick(group_of, group_b2)
    middle = residual_in + group_out + group_bias
    shared_in = layer_norm(middle, shared_gain).astype(bf16)

    def shared_first(block):
        return tuple(
            down(jax.nn.relu(jnp.dot(block, w, preferred_element_type=jnp.float32) + b))
            for w, b in ((shared_w1, shared_b1), (sw1_pair, sb1_pair))
        )

    def shared_second(hidden):
        return down(
            jnp.dot(hidden[0], shared_w2, preferred_element_type=jnp.float32)
            + jnp.dot(hidden[1], sw2_pair, preferred_element_type=jnp.float32)
        )

    half_tok = tok_dev // 2
    one, two = shared_in[:half_tok], shared_in[half_tok:]
    prev, foll = shift(one, "y", 1), shift(one, "y", -1)
    far = shift(prev, "y", 1)
    first = jnp.concatenate([one, prev, foll, far], axis=0)
    held, _, _ = hold(two, prev, foll)
    foll = shift(held, "y", -1)
    held, _ = hold(two, far)
    prev = shift(held, "y", 1)
    far = shift(foll, "y", -1)
    other = jnp.concatenate([two, prev, foll, far], axis=0)
    *hidden, _ = hold(*shared_first(first), foll)
    own, prev, foll, via = jnp.split(shared_second(hidden), 4)
    via = shift(via, "y", -1)
    foll = shift(foll, "y", 1)
    prev = down(up(prev) + up(via))
    *hidden, prev_out, foll = hold(*shared_first(other), prev, foll)
    first = up(own) + up(shift(prev_out, "y", -1)) + up(foll)
    other = ring_scatter(*jnp.split(shared_second(hidden), 4), "y", -1)
    shared_out = jnp.concatenate([first, other], axis=0)
    return (middle + shared_out + shared_b2).astype(bf16)


def solution(mesh):
    chips = Mesh(mesh.devices.reshape(4, 2, 4, 2, 2), ("y", "core", "z", "xh", "xl"))
    group = ("y", "core")
    within = ("z", "xh", "xl")
    both = group + within
    placed = (
        P(both, None),
        P(both),
        P(),
        P(),
        P(group, None, within),
        P(group, within),
        P(group, within, None),
        P(),
        P(),
        P(None, group),
        P(group),
        P(group, None),
        P(),
    )
    return jax.shard_map(
        on_device,
        mesh=chips,
        in_specs=placed,
        out_specs=P(both, None),
        check_vma=False,
    )
```

```python
import jax
import jax.numpy as jnp
from jax import lax
from jax.experimental import pallas as pl
from jax.experimental.pallas import tpu as pltpu
from jax.sharding import Mesh, PartitionSpec as P

X = ("xh", "xl")


def layer_norm(values, gains):
    centre = jnp.mean(values, axis=-1, keepdims=True)
    centred = values - centre
    spread = jnp.mean(centred * centred, axis=-1, keepdims=True)
    return centred * lax.rsqrt(spread + 1e-05) * gains


def shift(value, axis, step):
    size = lax.axis_size(axis)
    return lax.ppermute(value, axis, [(i, (i + step) % size) for i in range(size)])


def swap_column(value):
    return lax.ppermute(value, "xl", [(0, 1), (1, 0)])


def swap_blocks(value):
    return lax.ppermute(value, X, [(0, 3), (3, 0), (1, 2), (2, 1)])


def swap_core(value):
    return lax.ppermute(value, "core", [(0, 1), (1, 0)])


def up(value):
    return value.astype(jnp.float32)


def down(value):
    return value.astype(jnp.bfloat16)


def hold(*values):
    return lax.optimization_barrier(values)


def ring_scatter(own, prev, foll, far, axis, way):
    via = up(shift(far, axis, -way))
    if way == 1:
        prev = down(up(prev) + via)
    else:
        foll = down(up(foll) + via)
    return up(own) + up(shift(prev, axis, -1)) + up(shift(foll, axis, 1))


def on_chip(value):
    def copy(source, target):
        pltpu.sync_copy(source, target)

    return pl.pallas_call(
        copy,
        in_specs=[pl.BlockSpec(memory_space=pl.ANY)],
        out_specs=pl.BlockSpec(memory_space=pltpu.VMEM),
        out_shape=pltpu.VMEM(value.shape, value.dtype),
        compiler_params=pltpu.CompilerParams(vmem_limit_bytes=262144),
        name="on_chip",
    )(value)


def pick(index, table):
    rows = jnp.broadcast_to(table[0], (index.shape[0], table.shape[1]))
    for i in range(1, table.shape[0]):
        rows = jnp.where((index == i)[:, None], table[i], rows)
    return rows


def on_device(
    tokens,
    languages,
    lang_group,
    group_gain,
    group_w1,
    group_b1,
    group_w2,
    group_b2,
    shared_gain,
    shared_w1,
    shared_b1,
    shared_w2,
    shared_b2,
):
    tok_dev = tokens.shape[0]
    width_model = tokens.shape[1]
    num_groups = group_gain.shape[0]
    num_langs = lang_group.shape[0]
    capacity = 3 * tok_dev // (2 * num_groups)
    bf16 = jnp.bfloat16

    cut = 5 * width_model // 8
    left, right = group_w2[0, :, :cut], group_w2[0, :, cut:]
    w1_out, b1_pair = hold(group_w1[0], swap_blocks(group_b1[0]))
    w1_pair = swap_blocks(w1_out)

    residual_in = tokens.astype(jnp.float32)
    lang_hit = (languages[:, None] == jnp.arange(num_langs, dtype=jnp.int32)[None, :]).astype(
        jnp.int32
    )
    group_of = jnp.sum(lang_hit * lang_group[None, :], axis=1)
    onehot = (group_of[:, None] == jnp.arange(num_groups, dtype=jnp.int32)[None, :]).astype(
        jnp.int32
    )
    earlier = jnp.cumsum(onehot, axis=0) - onehot
    slot_index = jnp.sum(earlier * onehot, axis=1)
    position = group_of * capacity + slot_index
    dispatch_map = (
        position[None, :] == jnp.arange(num_groups * capacity, dtype=jnp.int32)[:, None]
    ).astype(bf16)
    row_gains = pick(group_of, group_gain)
    normed = layer_norm(residual_in, row_gains).astype(bf16)
    outgoing = jnp.dot(dispatch_map, normed, preferred_element_type=jnp.float32).astype(bf16)
    count = num_groups * capacity // 2

    def exchange(value):
        value = value.reshape(num_groups, capacity, value.shape[-1])
        value = lax.all_to_all(value, ("y", "core"), split_axis=0, concat_axis=0, tiled=True)
        return value.reshape(2 * count, value.shape[-1])

    arrived, sw1_pair, sw2_pair, sb1_pair = hold(
        exchange(outgoing), swap_core(shared_w1), swap_core(shared_w2), swap_core(shared_b1)
    )
    a_own, b_own = arrived[:count], arrived[count:]
    a_prev, a_foll = shift(a_own, "z", 1), shift(a_own, "z", -1)
    a_far = shift(a_prev, "z", 1)
    b_pair = swap_column(b_own)
    a_near = jnp.concatenate([a_own, a_prev, a_foll], axis=0)
    a_near, b_pair = hold(a_near, b_pair)
    (b_own,) = hold(jnp.concatenate([b_own, b_pair], axis=0))
    b_foll = shift(b_own, "z", -1)
    held, a_far = hold(b_own, a_far)
    b_prev = shift(held, "z", 1)
    sw1_pair, sw2_pair, _ = hold(sw1_pair, sw2_pair, b_own)
    sw1_pair, sw2_pair = on_chip(sw1_pair), on_chip(sw2_pair)
    b_far = shift(b_foll, "z", -1)
    near_pair = swap_column(a_near)
    far_out, near_pair = hold(a_far, near_pair)
    far_pair = swap_column(far_out)
    left_out, _ = hold(left, a_far)
    w1_pair, near_pair, sw1_pair, sw2_pair = hold(w1_pair, near_pair, sw1_pair, sw2_pair)
    left_pair = swap_blocks(left_out)
    right_out, _ = hold(right, b_prev)
    right_pair = swap_blocks(right_out)
    w1 = jnp.concatenate([group_w1[0], w1_pair], axis=1)
    b1 = jnp.concatenate([group_b1[0], b1_pair])
    early = jnp.concatenate([a_near, a_far, b_own, b_foll, b_prev, near_pair], axis=0)
    late = jnp.concatenate([far_pair, b_far], axis=0)

    def first(rows):
        return down(jax.nn.relu(jnp.dot(rows, w1, preferred_element_type=jnp.float32) + b1))

    hidden = jnp.concatenate([first(early), first(late)], axis=0)

    def second(hidden, weight, weight_pair):
        weight = jnp.concatenate([weight, weight_pair], axis=0)
        return down(jnp.dot(hidden, weight, preferred_element_type=jnp.float32))

    def block(part, step):
        at = {"own": (0, 4, 10, 5), "prev": (1, 8, 11, 9), "foll": (2, 6, 12, 7), "far": (3, 14, 13, 15)}
        return jnp.concatenate([part[i * count : (i + 1) * count] for i in at[step]], axis=0)

    def ring(weight, weight_pair, hidden, way, after):
        part = second(hidden, weight, weight_pair)
        own, prev, foll = (block(part, step) for step in ("own", "prev", "foll"))
        via = shift(block(part, "far"), "z", -way)
        if way == 1:
            foll = shift(foll, "z", 1)
            via, foll, after = hold(via, foll, after)
            prev = down(up(prev) + up(via))
            hidden, prev = hold(hidden, prev)
            prev = shift(prev, "z", -1)
        else:
            prev = shift(prev, "z", -1)
            via, after = hold(via, after)
            foll = shift(down(up(foll) + up(via)), "z", 1)
        return up(own) + up(prev) + up(foll), hidden, after

    def finish(summed, back):
        return exchange(down(summed[: 2 * count] + up(back)))

    sum_l, hidden, right_pair = ring(left, left_pair, hidden, 1, right_pair)
    out_l = down(sum_l[2 * count :])
    back_l = swap_column(out_l)
    sum_r, _, back_l = ring(right, right_pair, hidden, -1, back_l)
    return_l = finish(sum_l, back_l)
    sum_r, return_l = hold(sum_r, return_l)
    back_r = swap_column(down(sum_r[2 * count :]))
    return_r = finish(sum_r, back_r)
    returned = jnp.concatenate([return_l, return_r], axis=1)
    group_out = lax.dot_general(
        dispatch_map, returned, (((0,), (0,)), ((), ())), preferred_element_type=jnp.float32
    )
    group_bias = pick(group_of, group_b2)
    middle = residual_in + group_out + group_bias
    shared_in = layer_norm(middle, shared_gain).astype(bf16)

    def shared_first(block):
        return tuple(
            down(jax.nn.relu(jnp.dot(block, w, preferred_element_type=jnp.float32) + b))
            for w, b in ((shared_w1, shared_b1), (sw1_pair, sb1_pair))
        )

    def shared_second(hidden):
        return down(
            jnp.dot(hidden[0], shared_w2, preferred_element_type=jnp.float32)
            + jnp.dot(hidden[1], sw2_pair, preferred_element_type=jnp.float32)
        )

    half_tok = tok_dev // 2
    one, two = shared_in[:half_tok], shared_in[half_tok:]
    prev, foll = shift(one, "y", 1), shift(one, "y", -1)
    far = shift(prev, "y", 1)
    first = jnp.concatenate([one, prev, foll, far], axis=0)
    held, _, _ = hold(two, prev, foll)
    foll = shift(held, "y", -1)
    held, _ = hold(two, far)
    prev = shift(held, "y", 1)
    far = shift(foll, "y", -1)
    other = jnp.concatenate([two, prev, foll, far], axis=0)
    *hidden, _ = hold(*shared_first(first), foll)
    own, prev, foll, via = jnp.split(shared_second(hidden), 4)
    via = shift(via, "y", -1)
    foll = shift(foll, "y", 1)
    prev = down(up(prev) + up(via))
    *hidden, prev_out, foll = hold(*shared_first(other), prev, foll)
    first = up(own) + up(shift(prev_out, "y", -1)) + up(foll)
    other = ring_scatter(*jnp.split(shared_second(hidden), 4), "y", -1)
    shared_out = jnp.concatenate([first, other], axis=0)
    return (middle + shared_out + shared_b2).astype(bf16)


def solution(mesh):
    chips = Mesh(mesh.devices.reshape(4, 2, 4, 2, 2), ("y", "core", "z", "xh", "xl"))
    group = ("y", "core")
    within = ("z", "xh", "xl")
    both = group + within
    placed = (
        P(both, None),
        P(both),
        P(),
        P(),
        P(group, None, within),
        P(group, within),
        P(group, within, None),
        P(),
        P(),
        P(None, group),
        P(group),
        P(group, None),
        P(),
    )
    return jax.shard_map(
        on_device,
        mesh=chips,
        in_specs=placed,
        out_specs=P(both, None),
        check_vma=False,
    )
```

```python
import jax
import jax.numpy as jnp
from jax import lax
from jax.experimental import pallas as pl
from jax.experimental.pallas import tpu as pltpu
from jax.sharding import Mesh, PartitionSpec as P

X = ("xh", "xl")


def layer_norm(values, gains):
    centre = jnp.mean(values, axis=-1, keepdims=True)
    centred = values - centre
    spread = jnp.mean(centred * centred, axis=-1, keepdims=True)
    return centred * lax.rsqrt(spread + 1e-05) * gains


def shift(value, axis, step):
    size = lax.axis_size(axis)
    return lax.ppermute(value, axis, [(i, (i + step) % size) for i in range(size)])


def swap_column(value):
    return lax.ppermute(value, "xl", [(0, 1), (1, 0)])


def swap_blocks(value):
    return lax.ppermute(value, X, [(0, 3), (3, 0), (1, 2), (2, 1)])


def swap_core(value):
    return lax.ppermute(value, "core", [(0, 1), (1, 0)])


def up(value):
    return value.astype(jnp.float32)


def down(value):
    return value.astype(jnp.bfloat16)


def hold(*values):
    return lax.optimization_barrier(values)


def ring_scatter(own, prev, foll, far, axis, way):
    via = up(shift(far, axis, -way))
    if way == 1:
        prev = down(up(prev) + via)
    else:
        foll = down(up(foll) + via)
    return up(own) + up(shift(prev, axis, -1)) + up(shift(foll, axis, 1))


def on_chip(value):
    def copy(source, target):
        pltpu.sync_copy(source, target)

    return pl.pallas_call(
        copy,
        in_specs=[pl.BlockSpec(memory_space=pl.ANY)],
        out_specs=pl.BlockSpec(memory_space=pltpu.VMEM),
        out_shape=pltpu.VMEM(value.shape, value.dtype),
        compiler_params=pltpu.CompilerParams(vmem_limit_bytes=262144),
        name="on_chip",
    )(value)


def pick(index, table):
    rows = jnp.broadcast_to(table[0], (index.shape[0], table.shape[1]))
    for i in range(1, table.shape[0]):
        rows = jnp.where((index == i)[:, None], table[i], rows)
    return rows


def on_device(
    tokens,
    languages,
    lang_group,
    group_gain,
    group_w1,
    group_b1,
    group_w2,
    group_b2,
    shared_gain,
    shared_w1,
    shared_b1,
    shared_w2,
    shared_b2,
):
    tok_dev = tokens.shape[0]
    width_model = tokens.shape[1]
    num_groups = group_gain.shape[0]
    num_langs = lang_group.shape[0]
    capacity = 3 * tok_dev // (2 * num_groups)
    bf16 = jnp.bfloat16

    cut = width_model // 2
    left, right = group_w2[0, :, :cut], group_w2[0, :, cut:]
    w1_out, b1_pair = hold(group_w1[0], swap_blocks(group_b1[0]))
    w1_pair = swap_blocks(w1_out)

    residual_in = tokens.astype(jnp.float32)
    lang_hit = (languages[:, None] == jnp.arange(num_langs, dtype=jnp.int32)[None, :]).astype(
        jnp.int32
    )
    group_of = jnp.sum(lang_hit * lang_group[None, :], axis=1)
    onehot = (group_of[:, None] == jnp.arange(num_groups, dtype=jnp.int32)[None, :]).astype(
        jnp.int32
    )
    earlier = jnp.cumsum(onehot, axis=0) - onehot
    slot_index = jnp.sum(earlier * onehot, axis=1)
    position = group_of * capacity + slot_index
    dispatch_map = (
        position[None, :] == jnp.arange(num_groups * capacity, dtype=jnp.int32)[:, None]
    ).astype(bf16)
    row_gains = pick(group_of, group_gain)
    normed = layer_norm(residual_in, row_gains).astype(bf16)
    outgoing = jnp.dot(dispatch_map, normed, preferred_element_type=jnp.float32).astype(bf16)
    count = num_groups * capacity // 2

    def exchange(value):
        value = value.reshape(num_groups, capacity, value.shape[-1])
        value = lax.all_to_all(value, ("y", "core"), split_axis=0, concat_axis=0, tiled=True)
        return value.reshape(2 * count, value.shape[-1])

    arrived, sw1_pair, sw2_pair, sb1_pair = hold(
        exchange(outgoing), swap_core(shared_w1), swap_core(shared_w2), swap_core(shared_b1)
    )
    a_own, b_own = arrived[:count], arrived[count:]
    a_prev, a_foll = shift(a_own, "z", 1), shift(a_own, "z", -1)
    a_far = shift(a_prev, "z", 1)
    b_pair = swap_column(b_own)
    a_near = jnp.concatenate([a_own, a_prev, a_foll], axis=0)
    a_near, b_pair = hold(a_near, b_pair)
    (b_own,) = hold(jnp.concatenate([b_own, b_pair], axis=0))
    b_foll = shift(b_own, "z", -1)
    held, a_far = hold(b_own, a_far)
    b_prev = shift(held, "z", 1)
    sw1_pair, sw2_pair, _ = hold(sw1_pair, sw2_pair, b_own)
    sw1_pair, sw2_pair = on_chip(sw1_pair), on_chip(sw2_pair)
    b_far = shift(b_foll, "z", -1)
    near_pair = swap_column(a_near)
    far_out, near_pair = hold(a_far, near_pair)
    far_pair = swap_column(far_out)
    left_out, _ = hold(left, a_far)
    w1_pair, near_pair, sw1_pair, sw2_pair = hold(w1_pair, near_pair, sw1_pair, sw2_pair)
    left_pair = swap_blocks(left_out)
    right_out, _ = hold(right, b_prev)
    right_pair = swap_blocks(right_out)
    w1 = jnp.concatenate([group_w1[0], w1_pair], axis=1)
    b1 = jnp.concatenate([group_b1[0], b1_pair])
    early = jnp.concatenate([a_near, a_far, b_own, b_foll, b_prev, near_pair], axis=0)
    late = jnp.concatenate([far_pair, b_far], axis=0)

    def first(rows):
        return down(jax.nn.relu(jnp.dot(rows, w1, preferred_element_type=jnp.float32) + b1))

    hidden = jnp.concatenate([first(early), first(late)], axis=0)

    def second(hidden, weight, weight_pair):
        weight = jnp.concatenate([weight, weight_pair], axis=0)
        return down(jnp.dot(hidden, weight, preferred_element_type=jnp.float32))

    def block(part, step):
        at = {"own": (0, 4, 10, 5), "prev": (1, 8, 11, 9), "foll": (2, 6, 12, 7), "far": (3, 14, 13, 15)}
        return jnp.concatenate([part[i * count : (i + 1) * count] for i in at[step]], axis=0)

    def ring(weight, weight_pair, hidden, way, after):
        part = second(hidden, weight, weight_pair)
        own, prev, foll = (block(part, step) for step in ("own", "prev", "foll"))
        via = shift(block(part, "far"), "z", -way)
        if way == 1:
            foll = shift(foll, "z", 1)
            via, foll, after = hold(via, foll, after)
            prev = down(up(prev) + up(via))
            hidden, prev = hold(hidden, prev)
            prev = shift(prev, "z", -1)
        else:
            prev = shift(prev, "z", -1)
            via, after = hold(via, after)
            foll = shift(down(up(foll) + up(via)), "z", 1)
        return up(own) + up(prev) + up(foll), hidden, after

    def finish(summed, back):
        return exchange(down(summed[: 2 * count] + up(back)))

    sum_l, hidden, right_pair = ring(left, left_pair, hidden, 1, right_pair)
    out_l = down(sum_l[2 * count :])
    back_l = swap_column(out_l)
    sum_r, _, back_l = ring(right, right_pair, hidden, -1, back_l)
    return_l = finish(sum_l, back_l)
    sum_r, return_l = hold(sum_r, return_l)
    back_r = swap_column(down(sum_r[2 * count :]))
    return_r = finish(sum_r, back_r)
    returned = jnp.concatenate([return_l, return_r], axis=1)
    group_out = lax.dot_general(
        dispatch_map, returned, (((0,), (0,)), ((), ())), preferred_element_type=jnp.float32
    )
    group_bias = pick(group_of, group_b2)
    middle = residual_in + group_out + group_bias
    shared_in = layer_norm(middle, shared_gain).astype(bf16)

    def shared_first(block):
        return tuple(
            down(jax.nn.relu(jnp.dot(block, w, preferred_element_type=jnp.float32) + b))
            for w, b in ((shared_w1, shared_b1), (sw1_pair, sb1_pair))
        )

    def shared_second(hidden):
        return down(
            jnp.dot(hidden[0], shared_w2, preferred_element_type=jnp.float32)
            + jnp.dot(hidden[1], sw2_pair, preferred_element_type=jnp.float32)
        )

    half_tok = tok_dev // 2
    one, two = shared_in[:half_tok], shared_in[half_tok:]
    prev, foll = shift(one, "y", 1), shift(one, "y", -1)
    far = shift(prev, "y", 1)
    first = jnp.concatenate([one, prev, foll, far], axis=0)
    held, _, _ = hold(two, prev, foll)
    foll = shift(held, "y", -1)
    held, _ = hold(two, far)
    prev = shift(held, "y", 1)
    far = shift(foll, "y", -1)
    other = jnp.concatenate([two, prev, foll, far], axis=0)
    *hidden, _ = hold(*shared_first(first), foll)
    own, prev, foll, via = jnp.split(shared_second(hidden), 4)
    via = shift(via, "y", -1)
    foll = shift(foll, "y", 1)
    prev = down(up(prev) + up(via))
    *hidden, prev_out, foll = hold(*shared_first(other), prev, foll)
    first = up(own) + up(shift(prev_out, "y", -1)) + up(foll)
    other = ring_scatter(*jnp.split(shared_second(hidden), 4), "y", -1)
    shared_out = jnp.concatenate([first, other], axis=0)
    return (middle + shared_out + shared_b2).astype(bf16)


def solution(mesh):
    chips = Mesh(mesh.devices.reshape(4, 2, 4, 2, 2), ("y", "core", "z", "xh", "xl"))
    group = ("y", "core")
    within = ("z", "xh", "xl")
    both = group + within
    placed = (
        P(both, None),
        P(both),
        P(),
        P(),
        P(group, None, within),
        P(group, within),
        P(group, within, None),
        P(),
        P(),
        P(None, group),
        P(group),
        P(group, None),
        P(),
    )
    return jax.shard_map(
        on_device,
        mesh=chips,
        in_specs=placed,
        out_specs=P(both, None),
        check_vma=False,
    )
```

```python
import jax
import jax.numpy as jnp
from jax import lax
from jax.experimental import pallas as pl
from jax.experimental.pallas import tpu as pltpu
from jax.sharding import Mesh, PartitionSpec as P

X = ("xh", "xl")


def layer_norm(values, gains):
    centre = jnp.mean(values, axis=-1, keepdims=True)
    centred = values - centre
    spread = jnp.mean(centred * centred, axis=-1, keepdims=True)
    return centred * lax.rsqrt(spread + 1e-05) * gains


def shift(value, axis, step):
    size = lax.axis_size(axis)
    return lax.ppermute(value, axis, [(i, (i + step) % size) for i in range(size)])


def swap_column(value):
    return lax.ppermute(value, "xl", [(0, 1), (1, 0)])


def swap_blocks(value):
    return lax.ppermute(value, X, [(0, 3), (3, 0), (1, 2), (2, 1)])


def swap_core(value):
    return lax.ppermute(value, "core", [(0, 1), (1, 0)])


def up(value):
    return value.astype(jnp.float32)


def down(value):
    return value.astype(jnp.bfloat16)


def hold(*values):
    return lax.optimization_barrier(values)


def ring_scatter(own, prev, foll, far, axis, way):
    via = up(shift(far, axis, -way))
    if way == 1:
        prev = down(up(prev) + via)
    else:
        foll = down(up(foll) + via)
    return up(own) + up(shift(prev, axis, -1)) + up(shift(foll, axis, 1))


def dispatch(tokens, group_of, group_gain, capacity):
    num_tok, width = tokens.shape
    num_groups = group_gain.shape[0]
    num_slots = num_groups * capacity

    def body(tokens_ref, group_ref, gain_ref, out_ref, position_ref, rows_ref):
        group = group_ref[...]
        member = (lax.broadcasted_iota(jnp.int32, (num_groups, num_tok), 0) == group).astype(
            jnp.float32
        )
        before = (
            lax.broadcasted_iota(jnp.int32, (num_tok, num_tok), 0)
            < lax.broadcasted_iota(jnp.int32, (num_tok, num_tok), 1)
        ).astype(jnp.float32)
        earlier = jnp.dot(
            member.astype(jnp.bfloat16),
            before.astype(jnp.bfloat16),
            preferred_element_type=jnp.float32,
        )
        slot = jnp.sum(earlier * member, axis=0, keepdims=True)
        position = group * capacity + slot.astype(jnp.int32)
        position_ref[...] = position
        chosen = lax.broadcasted_iota(jnp.int32, (num_slots, num_tok), 0) == position
        rows_ref[...] = jnp.dot(
            chosen.astype(jnp.float32).astype(jnp.bfloat16),
            tokens_ref[...],
            preferred_element_type=jnp.float32,
        )
        for start in range(0, num_slots, 16):
            rows = rows_ref[start : start + 16]
            gains = [
                jnp.broadcast_to(gain_ref[at // capacity : at // capacity + 1], (8, width))
                for at in (start, start + 8)
            ]
            normed = layer_norm(rows, jnp.concatenate(gains, axis=0))
            out_ref[start : start + 16] = normed.astype(jnp.bfloat16)

    outgoing, position = pl.pallas_call(
        body,
        in_specs=[pl.BlockSpec(memory_space=pltpu.VMEM)] * 3,
        out_specs=[pl.BlockSpec(memory_space=pltpu.VMEM)] * 2,
        out_shape=[
            jax.ShapeDtypeStruct((num_slots, width), jnp.bfloat16),
            jax.ShapeDtypeStruct((1, num_tok), jnp.int32),
        ],
        scratch_shapes=[pltpu.VMEM((num_slots, width), jnp.float32)],
        compiler_params=pltpu.CompilerParams(vmem_limit_bytes=16 * 1024 * 1024),
        name="dispatch",
    )(tokens, group_of.reshape(1, num_tok), group_gain)
    return outgoing, position[0]


def on_chip(value):
    def copy(source, target):
        pltpu.sync_copy(source, target)

    return pl.pallas_call(
        copy,
        in_specs=[pl.BlockSpec(memory_space=pl.ANY)],
        out_specs=pl.BlockSpec(memory_space=pltpu.VMEM),
        out_shape=pltpu.VMEM(value.shape, value.dtype),
        compiler_params=pltpu.CompilerParams(vmem_limit_bytes=262144),
        name="on_chip",
    )(value)


def pick(index, table):
    rows = jnp.broadcast_to(table[0], (index.shape[0], table.shape[1]))
    for i in range(1, table.shape[0]):
        rows = jnp.where((index == i)[:, None], table[i], rows)
    return rows


def on_device(
    tokens,
    languages,
    lang_group,
    group_gain,
    group_w1,
    group_b1,
    group_w2,
    group_b2,
    shared_gain,
    shared_w1,
    shared_b1,
    shared_w2,
    shared_b2,
):
    tok_dev = tokens.shape[0]
    width_model = tokens.shape[1]
    num_groups = group_gain.shape[0]
    num_langs = lang_group.shape[0]
    capacity = 3 * tok_dev // (2 * num_groups)
    bf16 = jnp.bfloat16

    cut = width_model // 2
    left, right = group_w2[0, :, :cut], group_w2[0, :, cut:]
    w1_out, b1_pair = hold(group_w1[0], swap_blocks(group_b1[0]))
    w1_pair = swap_blocks(w1_out)

    residual_in = tokens.astype(jnp.float32)
    lang_hit = (languages[:, None] == jnp.arange(num_langs, dtype=jnp.int32)[None, :]).astype(
        jnp.int32
    )
    group_of = jnp.sum(lang_hit * lang_group[None, :], axis=1)
    outgoing, position = dispatch(tokens, group_of, group_gain, capacity)
    dispatch_map = (
        position[None, :] == jnp.arange(num_groups * capacity, dtype=jnp.int32)[:, None]
    ).astype(bf16)
    count = num_groups * capacity // 2

    def exchange(value):
        value = value.reshape(num_groups, capacity, value.shape[-1])
        value = lax.all_to_all(value, ("y", "core"), split_axis=0, concat_axis=0, tiled=True)
        return value.reshape(2 * count, value.shape[-1])

    arrived, sw1_pair, sw2_pair, sb1_pair = hold(
        exchange(outgoing), swap_core(shared_w1), swap_core(shared_w2), swap_core(shared_b1)
    )
    a_own, b_own = arrived[:count], arrived[count:]
    a_prev, a_foll = shift(a_own, "z", 1), shift(a_own, "z", -1)
    a_far = shift(a_prev, "z", 1)
    b_pair = swap_column(b_own)
    a_near = jnp.concatenate([a_own, a_prev, a_foll], axis=0)
    a_near, b_pair = hold(a_near, b_pair)
    (b_own,) = hold(jnp.concatenate([b_own, b_pair], axis=0))
    b_foll = shift(b_own, "z", -1)
    held, a_far = hold(b_own, a_far)
    b_prev = shift(held, "z", 1)
    sw1_pair, sw2_pair, _ = hold(sw1_pair, sw2_pair, b_own)
    sw1_pair, sw2_pair = on_chip(sw1_pair), on_chip(sw2_pair)
    b_far = shift(b_foll, "z", -1)
    near_pair = swap_column(a_near)
    far_out, near_pair = hold(a_far, near_pair)
    far_pair = swap_column(far_out)
    left_out, _ = hold(left, a_far)
    w1_pair, near_pair, sw1_pair, sw2_pair = hold(w1_pair, near_pair, sw1_pair, sw2_pair)
    left_pair = swap_blocks(left_out)
    right_out, _ = hold(right, b_prev)
    right_pair = swap_blocks(right_out)
    w1 = jnp.concatenate([group_w1[0], w1_pair], axis=1)
    b1 = jnp.concatenate([group_b1[0], b1_pair])
    early = jnp.concatenate([a_near, a_far, b_own, b_foll, b_prev, near_pair], axis=0)
    late = jnp.concatenate([far_pair, b_far], axis=0)

    def first(rows):
        return down(jax.nn.relu(jnp.dot(rows, w1, preferred_element_type=jnp.float32) + b1))

    hidden = jnp.concatenate([first(early), first(late)], axis=0)

    def second(hidden, weight, weight_pair):
        weight = jnp.concatenate([weight, weight_pair], axis=0)
        return down(jnp.dot(hidden, weight, preferred_element_type=jnp.float32))

    def block(part, step):
        at = {"own": (0, 4, 10, 5), "prev": (1, 8, 11, 9), "foll": (2, 6, 12, 7), "far": (3, 14, 13, 15)}
        return jnp.concatenate([part[i * count : (i + 1) * count] for i in at[step]], axis=0)

    def ring(weight, weight_pair, hidden, way, after):
        part = second(hidden, weight, weight_pair)
        own, prev, foll = (block(part, step) for step in ("own", "prev", "foll"))
        via = shift(block(part, "far"), "z", -way)
        if way == 1:
            foll = shift(foll, "z", 1)
            via, foll, after = hold(via, foll, after)
            prev = down(up(prev) + up(via))
            hidden, prev = hold(hidden, prev)
            prev = shift(prev, "z", -1)
        else:
            prev = shift(prev, "z", -1)
            via, after = hold(via, after)
            foll = shift(down(up(foll) + up(via)), "z", 1)
        return up(own) + up(prev) + up(foll), hidden, after

    def finish(summed, back):
        return exchange(down(summed[: 2 * count] + up(back)))

    sum_l, hidden, right_pair = ring(left, left_pair, hidden, 1, right_pair)
    out_l = down(sum_l[2 * count :])
    back_l = swap_column(out_l)
    sum_r, _, back_l = ring(right, right_pair, hidden, -1, back_l)
    return_l = finish(sum_l, back_l)
    sum_r, return_l = hold(sum_r, return_l)
    back_r = swap_column(down(sum_r[2 * count :]))
    return_r = finish(sum_r, back_r)
    returned = jnp.concatenate([return_l, return_r], axis=1)
    group_out = lax.dot_general(
        dispatch_map, returned, (((0,), (0,)), ((), ())), preferred_element_type=jnp.float32
    )
    group_bias = pick(group_of, group_b2)
    middle = residual_in + group_out + group_bias
    shared_in = layer_norm(middle, shared_gain).astype(bf16)

    def shared_first(block):
        return tuple(
            down(jax.nn.relu(jnp.dot(block, w, preferred_element_type=jnp.float32) + b))
            for w, b in ((shared_w1, shared_b1), (sw1_pair, sb1_pair))
        )

    def shared_second(hidden):
        return down(
            jnp.dot(hidden[0], shared_w2, preferred_element_type=jnp.float32)
            + jnp.dot(hidden[1], sw2_pair, preferred_element_type=jnp.float32)
        )

    half_tok = tok_dev // 2
    one, two = shared_in[:half_tok], shared_in[half_tok:]
    prev, foll = shift(one, "y", 1), shift(one, "y", -1)
    far = shift(prev, "y", 1)
    first = jnp.concatenate([one, prev, foll, far], axis=0)
    held, _, _ = hold(two, prev, foll)
    foll = shift(held, "y", -1)
    held, _ = hold(two, far)
    prev = shift(held, "y", 1)
    far = shift(foll, "y", -1)
    other = jnp.concatenate([two, prev, foll, far], axis=0)
    *hidden, _ = hold(*shared_first(first), foll)
    own, prev, foll, via = jnp.split(shared_second(hidden), 4)
    via = shift(via, "y", -1)
    foll = shift(foll, "y", 1)
    prev = down(up(prev) + up(via))
    *hidden, prev_out, foll = hold(*shared_first(other), prev, foll)
    first = up(own) + up(shift(prev_out, "y", -1)) + up(foll)
    other = ring_scatter(*jnp.split(shared_second(hidden), 4), "y", -1)
    shared_out = jnp.concatenate([first, other], axis=0)
    return (middle + shared_out + shared_b2).astype(bf16)


def solution(mesh):
    chips = Mesh(mesh.devices.reshape(4, 2, 4, 2, 2), ("y", "core", "z", "xh", "xl"))
    group = ("y", "core")
    within = ("z", "xh", "xl")
    both = group + within
    placed = (
        P(both, None),
        P(both),
        P(),
        P(),
        P(group, None, within),
        P(group, within),
        P(group, within, None),
        P(),
        P(),
        P(None, group),
        P(group),
        P(group, None),
        P(),
    )
    return jax.shard_map(
        on_device,
        mesh=chips,
        in_specs=placed,
        out_specs=P(both, None),
        check_vma=False,
    )
```

```python
import jax
import jax.numpy as jnp
from jax import lax
from jax.experimental import pallas as pl
from jax.experimental.pallas import tpu as pltpu
from jax.sharding import Mesh, PartitionSpec as P

X = ("xh", "xl")


def layer_norm(values, gains):
    centre = jnp.mean(values, axis=-1, keepdims=True)
    centred = values - centre
    spread = jnp.mean(centred * centred, axis=-1, keepdims=True)
    return centred * lax.rsqrt(spread + 1e-05) * gains


def shift(value, axis, step):
    size = lax.axis_size(axis)
    return lax.ppermute(value, axis, [(i, (i + step) % size) for i in range(size)])


def swap_column(value):
    return lax.ppermute(value, "xl", [(0, 1), (1, 0)])


def swap_blocks(value):
    return lax.ppermute(value, X, [(0, 3), (3, 0), (1, 2), (2, 1)])


def swap_core(value):
    return lax.ppermute(value, "core", [(0, 1), (1, 0)])


def up(value):
    return value.astype(jnp.float32)


def down(value):
    return value.astype(jnp.bfloat16)


def hold(*values):
    return lax.optimization_barrier(values)


def ring_scatter(own, prev, foll, far, axis, way):
    via = up(shift(far, axis, -way))
    if way == 1:
        prev = down(up(prev) + via)
    else:
        foll = down(up(foll) + via)
    return up(own) + up(shift(prev, axis, -1)) + up(shift(foll, axis, 1))


def dispatch(tokens, group_of, group_gain, capacity):
    num_tok, width = tokens.shape
    num_groups = group_gain.shape[0]
    num_slots = num_groups * capacity

    def body(tokens_ref, group_ref, gain_ref, out_ref, position_ref, rows_ref):
        group = group_ref[...]
        member = (lax.broadcasted_iota(jnp.int32, (num_groups, num_tok), 0) == group).astype(
            jnp.float32
        )
        before = (
            lax.broadcasted_iota(jnp.int32, (num_tok, num_tok), 0)
            < lax.broadcasted_iota(jnp.int32, (num_tok, num_tok), 1)
        ).astype(jnp.float32)
        earlier = jnp.dot(
            member.astype(jnp.bfloat16),
            before.astype(jnp.bfloat16),
            preferred_element_type=jnp.float32,
        )
        slot = jnp.sum(earlier * member, axis=0, keepdims=True)
        position = group * capacity + slot.astype(jnp.int32)
        position_ref[...] = position
        chosen = lax.broadcasted_iota(jnp.int32, (num_slots, num_tok), 0) == position
        rows_ref[...] = jnp.dot(
            chosen.astype(jnp.float32).astype(jnp.bfloat16),
            tokens_ref[...],
            preferred_element_type=jnp.float32,
        )
        for start in range(0, num_slots, 16):
            rows = rows_ref[start : start + 16]
            gains = [
                jnp.broadcast_to(gain_ref[at // capacity : at // capacity + 1], (8, width))
                for at in (start, start + 8)
            ]
            normed = layer_norm(rows, jnp.concatenate(gains, axis=0))
            out_ref[start : start + 16] = normed.astype(jnp.bfloat16)

    outgoing, position = pl.pallas_call(
        body,
        in_specs=[pl.BlockSpec(memory_space=pltpu.VMEM)] * 3,
        out_specs=[pl.BlockSpec(memory_space=pltpu.VMEM)] * 2,
        out_shape=[
            jax.ShapeDtypeStruct((num_slots, width), jnp.bfloat16),
            jax.ShapeDtypeStruct((1, num_tok), jnp.int32),
        ],
        scratch_shapes=[pltpu.VMEM((num_slots, width), jnp.float32)],
        compiler_params=pltpu.CompilerParams(vmem_limit_bytes=16 * 1024 * 1024),
        name="dispatch",
    )(tokens, group_of.reshape(1, num_tok), group_gain)
    return outgoing, position[0]


def on_chip(value):
    def copy(source, target):
        pltpu.sync_copy(source, target)

    return pl.pallas_call(
        copy,
        in_specs=[pl.BlockSpec(memory_space=pl.ANY)],
        out_specs=pl.BlockSpec(memory_space=pltpu.VMEM),
        out_shape=pltpu.VMEM(value.shape, value.dtype),
        compiler_params=pltpu.CompilerParams(vmem_limit_bytes=262144),
        name="on_chip",
    )(value)


def pick(index, table):
    rows = jnp.broadcast_to(table[0], (index.shape[0], table.shape[1]))
    for i in range(1, table.shape[0]):
        rows = jnp.where((index == i)[:, None], table[i], rows)
    return rows


def on_device(
    tokens,
    languages,
    lang_group,
    group_gain,
    group_w1,
    group_b1,
    group_w2,
    group_b2,
    shared_gain,
    shared_w1,
    shared_b1,
    shared_w2,
    shared_b2,
):
    tok_dev = tokens.shape[0]
    width_model = tokens.shape[1]
    num_groups = group_gain.shape[0]
    num_langs = lang_group.shape[0]
    capacity = 3 * tok_dev // (2 * num_groups)
    bf16 = jnp.bfloat16

    cut = width_model // 2
    left, right = group_w2[0, :, :cut], group_w2[0, :, cut:]
    w1_out, b1_pair = hold(group_w1[0], swap_blocks(group_b1[0]))
    w1_pair = swap_blocks(w1_out)

    residual_in = tokens.astype(jnp.float32)
    lang_hit = (languages[:, None] == jnp.arange(num_langs, dtype=jnp.int32)[None, :]).astype(
        jnp.int32
    )
    group_of = jnp.sum(lang_hit * lang_group[None, :], axis=1)
    outgoing, position = dispatch(tokens, group_of, group_gain, capacity)
    outgoing, b1_pair = hold(outgoing, b1_pair)
    dispatch_map = (
        position[None, :] == jnp.arange(num_groups * capacity, dtype=jnp.int32)[:, None]
    ).astype(bf16)
    count = num_groups * capacity // 2

    def exchange(value):
        value = value.reshape(num_groups, capacity, value.shape[-1])
        value = lax.all_to_all(value, ("y", "core"), split_axis=0, concat_axis=0, tiled=True)
        return value.reshape(2 * count, value.shape[-1])

    arrived, sw1_pair, sw2_pair, sb1_pair = hold(
        exchange(outgoing), swap_core(shared_w1), swap_core(shared_w2), swap_core(shared_b1)
    )
    a_own, b_own = arrived[:count], arrived[count:]
    a_prev, a_foll = shift(a_own, "z", 1), shift(a_own, "z", -1)
    a_far = shift(a_prev, "z", 1)
    b_pair = swap_column(b_own)
    a_near = jnp.concatenate([a_own, a_prev, a_foll], axis=0)
    a_near, b_pair = hold(a_near, b_pair)
    (b_own,) = hold(jnp.concatenate([b_own, b_pair], axis=0))
    b_foll = shift(b_own, "z", -1)
    held, a_far = hold(b_own, a_far)
    b_prev = shift(held, "z", 1)
    sw1_pair, sw2_pair, _ = hold(sw1_pair, sw2_pair, b_own)
    sw1_pair, sw2_pair = on_chip(sw1_pair), on_chip(sw2_pair)
    b_far = shift(b_foll, "z", -1)
    near_pair = swap_column(a_near)
    far_out, near_pair = hold(a_far, near_pair)
    far_pair = swap_column(far_out)
    left_out, _ = hold(left, a_far)
    w1_pair, near_pair, sw1_pair, sw2_pair = hold(w1_pair, near_pair, sw1_pair, sw2_pair)
    left_pair = swap_blocks(left_out)
    right_out, _ = hold(right, b_prev)
    right_pair = swap_blocks(right_out)
    w1 = jnp.concatenate([group_w1[0], w1_pair], axis=1)
    b1 = jnp.concatenate([group_b1[0], b1_pair])
    early = jnp.concatenate([a_near, a_far, b_own, b_foll, b_prev, near_pair], axis=0)
    late = jnp.concatenate([far_pair, b_far], axis=0)

    def first(rows):
        return down(jax.nn.relu(jnp.dot(rows, w1, preferred_element_type=jnp.float32) + b1))

    hidden = jnp.concatenate([first(early), first(late)], axis=0)

    def second(hidden, weight, weight_pair):
        weight = jnp.concatenate([weight, weight_pair], axis=0)
        return down(jnp.dot(hidden, weight, preferred_element_type=jnp.float32))

    def block(part, step):
        at = {"own": (0, 4, 10, 5), "prev": (1, 8, 11, 9), "foll": (2, 6, 12, 7), "far": (3, 14, 13, 15)}
        return jnp.concatenate([part[i * count : (i + 1) * count] for i in at[step]], axis=0)

    def ring(weight, weight_pair, hidden, way, after):
        part = second(hidden, weight, weight_pair)
        own, prev, foll = (block(part, step) for step in ("own", "prev", "foll"))
        via = shift(block(part, "far"), "z", -way)
        if way == 1:
            foll = shift(foll, "z", 1)
            via, foll, after = hold(via, foll, after)
            prev = down(up(prev) + up(via))
            hidden, prev = hold(hidden, prev)
            prev = shift(prev, "z", -1)
        else:
            prev = shift(prev, "z", -1)
            via, after = hold(via, after)
            foll = shift(down(up(foll) + up(via)), "z", 1)
        return up(own) + up(prev) + up(foll), hidden, after

    def finish(summed, back):
        return exchange(down(summed[: 2 * count] + up(back)))

    sum_l, hidden, right_pair = ring(left, left_pair, hidden, 1, right_pair)
    out_l = down(sum_l[2 * count :])
    back_l = swap_column(out_l)
    sum_r, _, back_l = ring(right, right_pair, hidden, -1, back_l)
    return_l = finish(sum_l, back_l)
    sum_r, return_l = hold(sum_r, return_l)
    back_r = swap_column(down(sum_r[2 * count :]))
    return_r = finish(sum_r, back_r)
    returned = jnp.concatenate([return_l, return_r], axis=1)
    group_out = lax.dot_general(
        dispatch_map, returned, (((0,), (0,)), ((), ())), preferred_element_type=jnp.float32
    )
    group_bias = pick(group_of, group_b2)
    middle = residual_in + group_out + group_bias
    shared_in = layer_norm(middle, shared_gain).astype(bf16)

    def shared_first(block):
        return tuple(
            down(jax.nn.relu(jnp.dot(block, w, preferred_element_type=jnp.float32) + b))
            for w, b in ((shared_w1, shared_b1), (sw1_pair, sb1_pair))
        )

    def shared_second(hidden):
        return down(
            jnp.dot(hidden[0], shared_w2, preferred_element_type=jnp.float32)
            + jnp.dot(hidden[1], sw2_pair, preferred_element_type=jnp.float32)
        )

    half_tok = tok_dev // 2
    one, two = shared_in[:half_tok], shared_in[half_tok:]
    prev, foll = shift(one, "y", 1), shift(one, "y", -1)
    far = shift(prev, "y", 1)
    first = jnp.concatenate([one, prev, foll, far], axis=0)
    held, _, _ = hold(two, prev, foll)
    foll = shift(held, "y", -1)
    held, _ = hold(two, far)
    prev = shift(held, "y", 1)
    far = shift(foll, "y", -1)
    other = jnp.concatenate([two, prev, foll, far], axis=0)
    *hidden, _ = hold(*shared_first(first), foll)
    own, prev, foll, via = jnp.split(shared_second(hidden), 4)
    via = shift(via, "y", -1)
    foll = shift(foll, "y", 1)
    prev = down(up(prev) + up(via))
    *hidden, prev_out, foll = hold(*shared_first(other), prev, foll)
    first = up(own) + up(shift(prev_out, "y", -1)) + up(foll)
    other = ring_scatter(*jnp.split(shared_second(hidden), 4), "y", -1)
    shared_out = jnp.concatenate([first, other], axis=0)
    return (middle + shared_out + shared_b2).astype(bf16)


def solution(mesh):
    chips = Mesh(mesh.devices.reshape(4, 2, 4, 2, 2), ("y", "core", "z", "xh", "xl"))
    group = ("y", "core")
    within = ("z", "xh", "xl")
    both = group + within
    placed = (
        P(both, None),
        P(both),
        P(),
        P(),
        P(group, None, within),
        P(group, within),
        P(group, within, None),
        P(),
        P(),
        P(None, group),
        P(group),
        P(group, None),
        P(),
    )
    return jax.shard_map(
        on_device,
        mesh=chips,
        in_specs=placed,
        out_specs=P(both, None),
        check_vma=False,
    )
```

```python
import jax
import jax.numpy as jnp
from jax import lax
from jax.experimental import pallas as pl
from jax.experimental.pallas import tpu as pltpu
from jax.sharding import Mesh, PartitionSpec as P

X = ("xh", "xl")


def layer_norm(values, gains):
    centre = jnp.mean(values, axis=-1, keepdims=True)
    centred = values - centre
    spread = jnp.mean(centred * centred, axis=-1, keepdims=True)
    return centred * lax.rsqrt(spread + 1e-05) * gains


def shift(value, axis, step):
    size = lax.axis_size(axis)
    return lax.ppermute(value, axis, [(i, (i + step) % size) for i in range(size)])


def swap_column(value):
    return lax.ppermute(value, "xl", [(0, 1), (1, 0)])


def swap_blocks(value):
    return lax.ppermute(value, X, [(0, 3), (3, 0), (1, 2), (2, 1)])


def swap_core(value):
    return lax.ppermute(value, "core", [(0, 1), (1, 0)])


def up(value):
    return value.astype(jnp.float32)


def down(value):
    return value.astype(jnp.bfloat16)


def hold(*values):
    return lax.optimization_barrier(values)


def ring_scatter(own, prev, foll, far, axis, way):
    via = up(shift(far, axis, -way))
    if way == 1:
        prev = down(up(prev) + via)
    else:
        foll = down(up(foll) + via)
    return up(own) + up(shift(prev, axis, -1)) + up(shift(foll, axis, 1))


def dispatch(tokens, group_of, group_gain, capacity):
    num_tok, width = tokens.shape
    num_groups = group_gain.shape[0]
    num_slots = num_groups * capacity

    def body(tokens_ref, group_ref, gain_ref, out_ref, position_ref, rows_ref):
        group = group_ref[...]
        member = (lax.broadcasted_iota(jnp.int32, (num_groups, num_tok), 0) == group).astype(
            jnp.float32
        )
        before = (
            lax.broadcasted_iota(jnp.int32, (num_tok, num_tok), 0)
            < lax.broadcasted_iota(jnp.int32, (num_tok, num_tok), 1)
        ).astype(jnp.float32)
        earlier = jnp.dot(
            member.astype(jnp.bfloat16),
            before.astype(jnp.bfloat16),
            preferred_element_type=jnp.float32,
        )
        slot = jnp.sum(earlier * member, axis=0, keepdims=True)
        position = group * capacity + slot.astype(jnp.int32)
        position_ref[...] = position
        chosen = lax.broadcasted_iota(jnp.int32, (num_slots, num_tok), 0) == position
        rows_ref[...] = jnp.dot(
            chosen.astype(jnp.float32).astype(jnp.bfloat16),
            tokens_ref[...],
            preferred_element_type=jnp.float32,
        )
        for start in range(0, num_slots, 16):
            rows = rows_ref[start : start + 16]
            gains = [
                jnp.broadcast_to(gain_ref[at // capacity : at // capacity + 1], (8, width))
                for at in (start, start + 8)
            ]
            normed = layer_norm(rows, jnp.concatenate(gains, axis=0))
            out_ref[start : start + 16] = normed.astype(jnp.bfloat16)

    outgoing, position = pl.pallas_call(
        body,
        in_specs=[pl.BlockSpec(memory_space=pltpu.VMEM)] * 3,
        out_specs=[pl.BlockSpec(memory_space=pltpu.VMEM)] * 2,
        out_shape=[
            jax.ShapeDtypeStruct((num_slots, width), jnp.bfloat16),
            jax.ShapeDtypeStruct((1, num_tok), jnp.int32),
        ],
        scratch_shapes=[pltpu.VMEM((num_slots, width), jnp.float32)],
        compiler_params=pltpu.CompilerParams(vmem_limit_bytes=16 * 1024 * 1024),
        name="dispatch",
    )(tokens, group_of.reshape(1, num_tok), group_gain)
    return outgoing, position[0]


def on_chip(value):
    def copy(source, target):
        pltpu.sync_copy(source, target)

    return pl.pallas_call(
        copy,
        in_specs=[pl.BlockSpec(memory_space=pl.ANY)],
        out_specs=pl.BlockSpec(memory_space=pltpu.VMEM),
        out_shape=pltpu.VMEM(value.shape, value.dtype),
        compiler_params=pltpu.CompilerParams(vmem_limit_bytes=262144),
        name="on_chip",
    )(value)


def pick(index, table):
    rows = jnp.broadcast_to(table[0], (index.shape[0], table.shape[1]))
    for i in range(1, table.shape[0]):
        rows = jnp.where((index == i)[:, None], table[i], rows)
    return rows


def on_device(
    tokens,
    languages,
    lang_group,
    group_gain,
    group_w1,
    group_b1,
    group_w2,
    group_b2,
    shared_gain,
    shared_w1,
    shared_b1,
    shared_w2,
    shared_b2,
):
    tok_dev = tokens.shape[0]
    width_model = tokens.shape[1]
    num_groups = group_gain.shape[0]
    num_langs = lang_group.shape[0]
    capacity = 3 * tok_dev // (2 * num_groups)
    bf16 = jnp.bfloat16

    cut = width_model // 2
    left, right = group_w2[0, :, :cut], group_w2[0, :, cut:]
    w1_out, b1_pair = hold(group_w1[0], swap_blocks(group_b1[0]))
    w1_pair = swap_blocks(w1_out)

    residual_in = tokens.astype(jnp.float32)
    lang_hit = (languages[:, None] == jnp.arange(num_langs, dtype=jnp.int32)[None, :]).astype(
        jnp.int32
    )
    group_of = jnp.sum(lang_hit * lang_group[None, :], axis=1)
    outgoing, position = dispatch(tokens, group_of, group_gain, capacity)
    dispatch_map = (
        position[None, :] == jnp.arange(num_groups * capacity, dtype=jnp.int32)[:, None]
    ).astype(bf16)
    count = num_groups * capacity // 2

    def exchange(value):
        value = value.reshape(num_groups, capacity, value.shape[-1])
        value = lax.all_to_all(value, ("y", "core"), split_axis=0, concat_axis=0, tiled=True)
        return value.reshape(2 * count, value.shape[-1])

    arrived, sw1_pair, sw2_pair, sb1_pair = hold(
        exchange(outgoing), swap_core(shared_w1), swap_core(shared_w2), swap_core(shared_b1)
    )
    a_own, b_own = arrived[:count], arrived[count:]
    a_prev, a_foll = shift(a_own, "z", 1), shift(a_own, "z", -1)
    a_far = shift(a_prev, "z", 1)
    b_pair = swap_column(b_own)
    a_near = jnp.concatenate([a_own, a_prev, a_foll], axis=0)
    a_near, b_pair = hold(a_near, b_pair)
    (b_own,) = hold(jnp.concatenate([b_own, b_pair], axis=0))
    b_foll = shift(b_own, "z", -1)
    held, a_far = hold(b_own, a_far)
    b_prev = shift(held, "z", 1)
    sw1_pair, sw2_pair, _ = hold(sw1_pair, sw2_pair, b_own)
    sw1_pair, sw2_pair = on_chip(sw1_pair), on_chip(sw2_pair)
    b_far = shift(b_foll, "z", -1)
    near_pair = swap_column(a_near)
    far_out, near_pair = hold(a_far, near_pair)
    far_pair = swap_column(far_out)
    left_out, _ = hold(left, a_far)
    w1_pair, near_pair, sw1_pair, sw2_pair = hold(w1_pair, near_pair, sw1_pair, sw2_pair)
    left_pair = swap_blocks(left_out)
    right_out, _ = hold(right, b_prev)
    right_pair = swap_blocks(right_out)
    w1 = jnp.concatenate([group_w1[0], w1_pair], axis=1)
    b1 = jnp.concatenate([group_b1[0], b1_pair])
    early = jnp.concatenate([a_near, a_far, b_own, b_foll, b_prev, near_pair], axis=0)
    late = jnp.concatenate([far_pair, b_far], axis=0)

    def first(rows):
        return down(jax.nn.relu(jnp.dot(rows, w1, preferred_element_type=jnp.float32) + b1))

    hidden = jnp.concatenate([first(early), first(late)], axis=0)

    def second(hidden, weight, weight_pair):
        weight = jnp.concatenate([weight, weight_pair], axis=0)
        return down(jnp.dot(hidden, weight, preferred_element_type=jnp.float32))

    def block(part, step):
        at = {"own": (0, 4, 10, 5), "prev": (1, 8, 11, 9), "foll": (2, 6, 12, 7), "far": (3, 14, 13, 15)}
        return jnp.concatenate([part[i * count : (i + 1) * count] for i in at[step]], axis=0)

    wide = 4 * count

    def ring(weight, weight_pair, hidden, way, after):
        part = second(hidden, weight, weight_pair)
        own, prev, foll = (block(part, step) for step in ("own", "prev", "foll"))
        via = shift(block(part, "far"), "z", -way)
        if way == 1:
            foll = shift(foll, "z", 1)
            via, foll, after = hold(via, foll, after)
            prev = down(up(prev) + up(via))
            hidden, prev = hold(hidden, prev)
            prev = shift(prev, "z", -1)
        else:
            prev = shift(prev, "z", -1)
            via, after = hold(via, after)
            foll = shift(down(up(foll) + up(via)), "z", 1)
        return up(own) + up(prev) + up(foll), hidden, after

    def finish(summed, back):
        return exchange(down(summed[: 2 * count] + up(back)))

    sum_l, hidden, right_pair = ring(left, left_pair, hidden, 1, right_pair)
    out_l = down(sum_l[2 * count :])
    back_l = swap_column(out_l)
    part = second(hidden, right, right_pair)
    back = swap_column(part[10 * count : 14 * count])
    via = shift(part[14 * count :], "z", 1)
    prev = shift(part[8 * count : 10 * count], "z", -1)
    foll = shift(down(up(part[6 * count : 8 * count]) + up(via)), "z", 1)
    sum_b = up(part[4 * count : 6 * count]) + up(prev) + up(foll)
    sum_b = sum_b[:count] + up(swap_column(down(sum_b[count:])))
    own, prev, foll, far = jnp.split(down(up(part[:wide]) + up(back)), 4)
    via = shift(far, "z", -1)
    foll = shift(foll, "z", 1)
    via, foll, back_l = hold(via, foll, back_l)
    return_l = finish(sum_l, back_l)
    prev = shift(down(up(prev) + up(via)), "z", -1)
    sum_b, return_l = hold(sum_b, return_l)
    sum_a = up(own) + up(prev) + up(foll)
    return_r = exchange(down(jnp.concatenate([sum_a, sum_b], axis=0)))
    returned = jnp.concatenate([return_l, return_r], axis=1)
    group_out = lax.dot_general(
        dispatch_map, returned, (((0,), (0,)), ((), ())), preferred_element_type=jnp.float32
    )
    group_bias = pick(group_of, group_b2)
    middle = residual_in + group_out + group_bias
    shared_in = layer_norm(middle, shared_gain).astype(bf16)

    def shared_first(block):
        return tuple(
            down(jax.nn.relu(jnp.dot(block, w, preferred_element_type=jnp.float32) + b))
            for w, b in ((shared_w1, shared_b1), (sw1_pair, sb1_pair))
        )

    def shared_second(hidden):
        return down(
            jnp.dot(hidden[0], shared_w2, preferred_element_type=jnp.float32)
            + jnp.dot(hidden[1], sw2_pair, preferred_element_type=jnp.float32)
        )

    half_tok = tok_dev // 2
    one, two = shared_in[:half_tok], shared_in[half_tok:]
    prev, foll = shift(one, "y", 1), shift(one, "y", -1)
    far = shift(prev, "y", 1)
    first = jnp.concatenate([one, prev, foll, far], axis=0)
    held, _, _ = hold(two, prev, foll)
    foll = shift(held, "y", -1)
    held, _ = hold(two, far)
    prev = shift(held, "y", 1)
    far = shift(foll, "y", -1)
    other = jnp.concatenate([two, prev, foll, far], axis=0)
    *hidden, _ = hold(*shared_first(first), foll)
    own, prev, foll, via = jnp.split(shared_second(hidden), 4)
    via = shift(via, "y", -1)
    foll = shift(foll, "y", 1)
    prev = down(up(prev) + up(via))
    *hidden, prev_out, foll = hold(*shared_first(other), prev, foll)
    first = up(own) + up(shift(prev_out, "y", -1)) + up(foll)
    other = ring_scatter(*jnp.split(shared_second(hidden), 4), "y", -1)
    shared_out = jnp.concatenate([first, other], axis=0)
    return (middle + shared_out + shared_b2).astype(bf16)


def solution(mesh):
    chips = Mesh(mesh.devices.reshape(4, 2, 4, 2, 2), ("y", "core", "z", "xh", "xl"))
    group = ("y", "core")
    within = ("z", "xh", "xl")
    both = group + within
    placed = (
        P(both, None),
        P(both),
        P(),
        P(),
        P(group, None, within),
        P(group, within),
        P(group, within, None),
        P(),
        P(),
        P(None, group),
        P(group),
        P(group, None),
        P(),
    )
    return jax.shard_map(
        on_device,
        mesh=chips,
        in_specs=placed,
        out_specs=P(both, None),
        check_vma=False,
    )
```

```python
import jax
import jax.numpy as jnp
from jax import lax
from jax.experimental import pallas as pl
from jax.experimental.pallas import tpu as pltpu
from jax.sharding import Mesh, PartitionSpec as P

X = ("xh", "xl")


def layer_norm(values, gains):
    centre = jnp.mean(values, axis=-1, keepdims=True)
    centred = values - centre
    spread = jnp.mean(centred * centred, axis=-1, keepdims=True)
    return centred * lax.rsqrt(spread + 1e-05) * gains


def shift(value, axis, step):
    size = lax.axis_size(axis)
    return lax.ppermute(value, axis, [(i, (i + step) % size) for i in range(size)])


def swap_column(value):
    return lax.ppermute(value, "xl", [(0, 1), (1, 0)])


def swap_blocks(value):
    return lax.ppermute(value, X, [(0, 3), (3, 0), (1, 2), (2, 1)])


def swap_core(value):
    return lax.ppermute(value, "core", [(0, 1), (1, 0)])


def up(value):
    return value.astype(jnp.float32)


def down(value):
    return value.astype(jnp.bfloat16)


def hold(*values):
    return lax.optimization_barrier(values)


def ring_scatter(own, prev, foll, far, axis, way):
    via = up(shift(far, axis, -way))
    if way == 1:
        prev = down(up(prev) + via)
    else:
        foll = down(up(foll) + via)
    return up(own) + up(shift(prev, axis, -1)) + up(shift(foll, axis, 1))


def dispatch(tokens, group_of, group_gain, capacity):
    num_tok, width = tokens.shape
    num_groups = group_gain.shape[0]
    num_slots = num_groups * capacity

    def body(tokens_ref, group_ref, gain_ref, out_ref, position_ref, rows_ref):
        group = group_ref[...]
        member = (lax.broadcasted_iota(jnp.int32, (num_groups, num_tok), 0) == group).astype(
            jnp.float32
        )
        before = (
            lax.broadcasted_iota(jnp.int32, (num_tok, num_tok), 0)
            < lax.broadcasted_iota(jnp.int32, (num_tok, num_tok), 1)
        ).astype(jnp.float32)
        earlier = jnp.dot(
            member.astype(jnp.bfloat16),
            before.astype(jnp.bfloat16),
            preferred_element_type=jnp.float32,
        )
        slot = jnp.sum(earlier * member, axis=0, keepdims=True)
        position = group * capacity + slot.astype(jnp.int32)
        position_ref[...] = position
        chosen = lax.broadcasted_iota(jnp.int32, (num_slots, num_tok), 0) == position
        rows_ref[...] = jnp.dot(
            chosen.astype(jnp.float32).astype(jnp.bfloat16),
            tokens_ref[...],
            preferred_element_type=jnp.float32,
        )

        def two_groups(pair, carry):
            for start in range(0, 2 * capacity, 16):
                at = pl.ds(pl.multiple_of(pair * 2 * capacity + start, 16), 16)
                gains = [
                    jnp.broadcast_to(gain_ref[pl.ds(2 * pair + row // capacity, 1)], (8, width))
                    for row in (start, start + 8)
                ]
                normed = layer_norm(rows_ref[at], jnp.concatenate(gains, axis=0))
                out_ref[at] = normed.astype(jnp.bfloat16)
            return carry

        lax.fori_loop(0, num_groups // 2, two_groups, 0)

    outgoing, position = pl.pallas_call(
        body,
        in_specs=[pl.BlockSpec(memory_space=pltpu.VMEM)] * 3,
        out_specs=[pl.BlockSpec(memory_space=pltpu.VMEM)] * 2,
        out_shape=[
            jax.ShapeDtypeStruct((num_slots, width), jnp.bfloat16),
            jax.ShapeDtypeStruct((1, num_tok), jnp.int32),
        ],
        scratch_shapes=[pltpu.VMEM((num_slots, width), jnp.float32)],
        compiler_params=pltpu.CompilerParams(vmem_limit_bytes=16 * 1024 * 1024),
        name="dispatch",
    )(tokens, group_of.reshape(1, num_tok), group_gain)
    return outgoing, position[0]


def on_chip(value):
    def copy(source, target):
        pltpu.sync_copy(source, target)

    return pl.pallas_call(
        copy,
        in_specs=[pl.BlockSpec(memory_space=pl.ANY)],
        out_specs=pl.BlockSpec(memory_space=pltpu.VMEM),
        out_shape=pltpu.VMEM(value.shape, value.dtype),
        compiler_params=pltpu.CompilerParams(vmem_limit_bytes=262144),
        name="on_chip",
    )(value)


def pick(index, table):
    rows = jnp.broadcast_to(table[0], (index.shape[0], table.shape[1]))
    for i in range(1, table.shape[0]):
        rows = jnp.where((index == i)[:, None], table[i], rows)
    return rows


def on_device(
    tokens,
    languages,
    lang_group,
    group_gain,
    group_w1,
    group_b1,
    group_w2,
    group_b2,
    shared_gain,
    shared_w1,
    shared_b1,
    shared_w2,
    shared_b2,
):
    tok_dev = tokens.shape[0]
    width_model = tokens.shape[1]
    num_groups = group_gain.shape[0]
    num_langs = lang_group.shape[0]
    capacity = 3 * tok_dev // (2 * num_groups)
    bf16 = jnp.bfloat16

    cut = width_model // 2
    left, right = group_w2[0, :, :cut], group_w2[0, :, cut:]
    w1_out, b1_pair = hold(group_w1[0], swap_blocks(group_b1[0]))
    w1_pair = swap_blocks(w1_out)

    residual_in = tokens.astype(jnp.float32)
    lang_hit = (languages[:, None] == jnp.arange(num_langs, dtype=jnp.int32)[None, :]).astype(
        jnp.int32
    )
    group_of = jnp.sum(lang_hit * lang_group[None, :], axis=1)
    outgoing, position = dispatch(tokens, group_of, group_gain, capacity)
    dispatch_map = (
        position[None, :] == jnp.arange(num_groups * capacity, dtype=jnp.int32)[:, None]
    ).astype(bf16)
    count = num_groups * capacity // 2

    def exchange(value):
        value = value.reshape(num_groups, capacity, value.shape[-1])
        value = lax.all_to_all(value, ("y", "core"), split_axis=0, concat_axis=0, tiled=True)
        return value.reshape(2 * count, value.shape[-1])

    arrived, sw1_pair, sw2_pair, sb1_pair = hold(
        exchange(outgoing), swap_core(shared_w1), swap_core(shared_w2), swap_core(shared_b1)
    )
    a_own, b_own = arrived[:count], arrived[count:]
    a_prev, a_foll = shift(a_own, "z", 1), shift(a_own, "z", -1)
    a_far = shift(a_prev, "z", 1)
    b_pair = swap_column(b_own)
    a_near = jnp.concatenate([a_own, a_prev, a_foll], axis=0)
    a_near, b_pair = hold(a_near, b_pair)
    (b_own,) = hold(jnp.concatenate([b_own, b_pair], axis=0))
    b_foll = shift(b_own, "z", -1)
    held, a_far = hold(b_own, a_far)
    b_prev = shift(held, "z", 1)
    sw1_pair, sw2_pair, _ = hold(sw1_pair, sw2_pair, b_own)
    sw1_pair, sw2_pair = on_chip(sw1_pair), on_chip(sw2_pair)
    b_far = shift(b_foll, "z", -1)
    near_pair = swap_column(a_near)
    far_out, near_pair = hold(a_far, near_pair)
    far_pair = swap_column(far_out)
    left_out, _ = hold(left, a_far)
    w1_pair, near_pair, sw1_pair, sw2_pair = hold(w1_pair, near_pair, sw1_pair, sw2_pair)
    left_pair = swap_blocks(left_out)
    right_out, _ = hold(right, b_prev)
    right_pair = swap_blocks(right_out)
    w1 = jnp.concatenate([group_w1[0], w1_pair], axis=1)
    b1 = jnp.concatenate([group_b1[0], b1_pair])
    rows = jnp.concatenate(
        [a_near, a_far, b_own, b_foll, b_prev, near_pair, far_pair, b_far], axis=0
    )
    hidden = down(jax.nn.relu(jnp.dot(rows, w1, preferred_element_type=jnp.float32) + b1))

    def second(hidden, weight, weight_pair):
        weight = jnp.concatenate([weight, weight_pair], axis=0)
        return down(jnp.dot(hidden, weight, preferred_element_type=jnp.float32))

    wide = 4 * count

    def open_half(weight, weight_pair, hidden):
        part = second(hidden, weight, weight_pair)
        back = swap_column(part[10 * count : 14 * count])
        via = shift(part[14 * count :], "z", 1)
        prev = shift(part[8 * count : 10 * count], "z", -1)
        foll = shift(down(up(part[6 * count : 8 * count]) + up(via)), "z", 1)
        sum_b = up(part[4 * count : 6 * count]) + up(prev) + up(foll)
        return part, back, sum_b[:count] + up(swap_column(down(sum_b[count:])))

    def close_half(rows, after):
        own, prev, foll, far = jnp.split(rows, 4)
        via = shift(far, "z", -1)
        foll = shift(foll, "z", 1)
        via, foll, after = hold(via, foll, after)
        prev = shift(down(up(prev) + up(via)), "z", -1)
        return up(own) + up(prev) + up(foll), after

    def finish(sum_a, sum_b):
        return exchange(down(jnp.concatenate([sum_a, sum_b], axis=0)))

    part, back, sum_b = open_half(left, left_pair, hidden)
    back, right_pair = hold(back, right_pair)
    rows = down(up(part[:wide]) + up(back))
    hidden, rows = hold(hidden, rows)
    sum_a, _ = close_half(rows, b1)
    return_l = finish(sum_a, sum_b)
    part, back, sum_b = open_half(right, right_pair, hidden)
    sum_a, return_l = close_half(down(up(part[:wide]) + up(back)), return_l)
    return_r = finish(sum_a, sum_b)
    returned = jnp.concatenate([return_l, return_r], axis=1)
    group_out = lax.dot_general(
        dispatch_map, returned, (((0,), (0,)), ((), ())), preferred_element_type=jnp.float32
    )
    group_bias = pick(group_of, group_b2)
    middle = residual_in + group_out + group_bias
    shared_in = layer_norm(middle, shared_gain).astype(bf16)

    def shared_first(block):
        return tuple(
            down(jax.nn.relu(jnp.dot(block, w, preferred_element_type=jnp.float32) + b))
            for w, b in ((shared_w1, shared_b1), (sw1_pair, sb1_pair))
        )

    def shared_second(hidden):
        return down(
            jnp.dot(hidden[0], shared_w2, preferred_element_type=jnp.float32)
            + jnp.dot(hidden[1], sw2_pair, preferred_element_type=jnp.float32)
        )

    half_tok = tok_dev // 2
    one, two = shared_in[:half_tok], shared_in[half_tok:]
    prev, foll = shift(one, "y", 1), shift(one, "y", -1)
    far = shift(prev, "y", 1)
    first = jnp.concatenate([one, prev, foll, far], axis=0)
    held, _, _ = hold(two, prev, foll)
    foll = shift(held, "y", -1)
    held, _ = hold(two, far)
    prev = shift(held, "y", 1)
    far = shift(foll, "y", -1)
    other = jnp.concatenate([two, prev, foll, far], axis=0)
    *hidden, _ = hold(*shared_first(first), foll)
    own, prev, foll, via = jnp.split(shared_second(hidden), 4)
    via = shift(via, "y", -1)
    foll = shift(foll, "y", 1)
    prev = down(up(prev) + up(via))
    *hidden, prev_out, foll = hold(*shared_first(other), prev, foll)
    first = up(own) + up(shift(prev_out, "y", -1)) + up(foll)
    other = ring_scatter(*jnp.split(shared_second(hidden), 4), "y", -1)
    shared_out = jnp.concatenate([first, other], axis=0)
    return (middle + shared_out + shared_b2).astype(bf16)


def solution(mesh):
    chips = Mesh(mesh.devices.reshape(4, 2, 4, 2, 2), ("y", "core", "z", "xh", "xl"))
    group = ("y", "core")
    within = ("z", "xh", "xl")
    both = group + within
    placed = (
        P(both, None),
        P(both),
        P(),
        P(),
        P(group, None, within),
        P(group, within),
        P(group, within, None),
        P(),
        P(),
        P(None, group),
        P(group),
        P(group, None),
        P(),
    )
    return jax.shard_map(
        on_device,
        mesh=chips,
        in_specs=placed,
        out_specs=P(both, None),
        check_vma=False,
    )
```

```python
import jax
import jax.numpy as jnp
from jax import lax
from jax.experimental import pallas as pl
from jax.experimental.pallas import tpu as pltpu
from jax.sharding import Mesh, PartitionSpec as P

X = ("xh", "xl")


def layer_norm(values, gains):
    centre = jnp.mean(values, axis=-1, keepdims=True)
    centred = values - centre
    spread = jnp.mean(centred * centred, axis=-1, keepdims=True)
    return centred * lax.rsqrt(spread + 1e-05) * gains


def shift(value, axis, step):
    size = lax.axis_size(axis)
    return lax.ppermute(value, axis, [(i, (i + step) % size) for i in range(size)])


def swap_column(value):
    return lax.ppermute(value, "xl", [(0, 1), (1, 0)])


def swap_blocks(value):
    return lax.ppermute(value, X, [(0, 3), (3, 0), (1, 2), (2, 1)])


def swap_core(value):
    return lax.ppermute(value, "core", [(0, 1), (1, 0)])


def up(value):
    return value.astype(jnp.float32)


def down(value):
    return value.astype(jnp.bfloat16)


def hold(*values):
    return lax.optimization_barrier(values)


def ring_scatter(own, prev, foll, far, axis, way):
    via = up(shift(far, axis, -way))
    if way == 1:
        prev = down(up(prev) + via)
    else:
        foll = down(up(foll) + via)
    return up(own) + up(shift(prev, axis, -1)) + up(shift(foll, axis, 1))


def dispatch(tokens, group_of, group_gain, capacity):
    num_tok, width = tokens.shape
    num_groups = group_gain.shape[0]
    num_slots = num_groups * capacity

    def body(tokens_ref, group_ref, gain_ref, out_ref, position_ref, rows_ref):
        group = group_ref[...]
        member = (lax.broadcasted_iota(jnp.int32, (num_groups, num_tok), 0) == group).astype(
            jnp.float32
        )
        before = (
            lax.broadcasted_iota(jnp.int32, (num_tok, num_tok), 0)
            < lax.broadcasted_iota(jnp.int32, (num_tok, num_tok), 1)
        ).astype(jnp.float32)
        earlier = jnp.dot(
            member.astype(jnp.bfloat16),
            before.astype(jnp.bfloat16),
            preferred_element_type=jnp.float32,
        )
        slot = jnp.sum(earlier * member, axis=0, keepdims=True)
        position = group * capacity + slot.astype(jnp.int32)
        position_ref[...] = position
        chosen = lax.broadcasted_iota(jnp.int32, (num_slots, num_tok), 0) == position
        rows_ref[...] = jnp.dot(
            chosen.astype(jnp.float32).astype(jnp.bfloat16),
            tokens_ref[...],
            preferred_element_type=jnp.float32,
        )
        for start in range(0, num_slots, 16):
            rows = rows_ref[start : start + 16]
            gains = [
                jnp.broadcast_to(gain_ref[at // capacity : at // capacity + 1], (8, width))
                for at in (start, start + 8)
            ]
            normed = layer_norm(rows, jnp.concatenate(gains, axis=0))
            out_ref[start : start + 16] = normed.astype(jnp.bfloat16)

    outgoing, position = pl.pallas_call(
        body,
        in_specs=[pl.BlockSpec(memory_space=pltpu.VMEM)] * 3,
        out_specs=[pl.BlockSpec(memory_space=pltpu.VMEM)] * 2,
        out_shape=[
            jax.ShapeDtypeStruct((num_slots, width), jnp.bfloat16),
            jax.ShapeDtypeStruct((1, num_tok), jnp.int32),
        ],
        scratch_shapes=[pltpu.VMEM((num_slots, width), jnp.float32)],
        compiler_params=pltpu.CompilerParams(vmem_limit_bytes=16 * 1024 * 1024),
        name="dispatch",
    )(tokens, group_of.reshape(1, num_tok), group_gain)
    return outgoing, position[0]


def on_chip(value):
    def copy(source, target):
        pltpu.sync_copy(source, target)

    return pl.pallas_call(
        copy,
        in_specs=[pl.BlockSpec(memory_space=pl.ANY)],
        out_specs=pl.BlockSpec(memory_space=pltpu.VMEM),
        out_shape=pltpu.VMEM(value.shape, value.dtype),
        compiler_params=pltpu.CompilerParams(vmem_limit_bytes=262144),
        name="on_chip",
    )(value)


def pick(index, table):
    rows = jnp.broadcast_to(table[0], (index.shape[0], table.shape[1]))
    for i in range(1, table.shape[0]):
        rows = jnp.where((index == i)[:, None], table[i], rows)
    return rows


def on_device(
    tokens,
    languages,
    lang_group,
    group_gain,
    group_w1,
    group_b1,
    group_w2,
    group_b2,
    shared_gain,
    shared_w1,
    shared_b1,
    shared_w2,
    shared_b2,
):
    tok_dev = tokens.shape[0]
    width_model = tokens.shape[1]
    num_groups = group_gain.shape[0]
    num_langs = lang_group.shape[0]
    capacity = 3 * tok_dev // (2 * num_groups)
    bf16 = jnp.bfloat16

    cut = width_model // 2
    left, right = group_w2[0, :, :cut], group_w2[0, :, cut:]
    w1_out, b1_pair = hold(group_w1[0], swap_blocks(group_b1[0]))
    w1_pair = swap_blocks(w1_out)

    residual_in = tokens.astype(jnp.float32)
    lang_hit = (languages[:, None] == jnp.arange(num_langs, dtype=jnp.int32)[None, :]).astype(
        jnp.int32
    )
    group_of = jnp.sum(lang_hit * lang_group[None, :], axis=1)
    outgoing, position = dispatch(tokens, group_of, group_gain, capacity)
    dispatch_map = (
        position[None, :] == jnp.arange(num_groups * capacity, dtype=jnp.int32)[:, None]
    ).astype(bf16)
    count = num_groups * capacity // 2

    def exchange(value):
        value = value.reshape(num_groups, capacity, value.shape[-1])
        value = lax.all_to_all(value, ("y", "core"), split_axis=0, concat_axis=0, tiled=True)
        return value.reshape(2 * count, value.shape[-1])

    arrived, sw1_pair, sw2_pair, sb1_pair = hold(
        exchange(outgoing), swap_core(shared_w1), swap_core(shared_w2), swap_core(shared_b1)
    )
    a_own, b_own = arrived[:count], arrived[count:]
    a_prev, a_foll = shift(a_own, "z", 1), shift(a_own, "z", -1)
    a_far = shift(a_prev, "z", 1)
    b_pair = swap_column(b_own)
    a_near = jnp.concatenate([a_own, a_prev, a_foll], axis=0)
    a_near, b_pair = hold(a_near, b_pair)
    (b_own,) = hold(jnp.concatenate([b_own, b_pair], axis=0))
    b_foll = shift(b_own, "z", -1)
    held, a_far = hold(b_own, a_far)
    b_prev = shift(held, "z", 1)
    sw1_pair, sw2_pair, _ = hold(sw1_pair, sw2_pair, b_own)
    sw1_pair, sw2_pair = on_chip(sw1_pair), on_chip(sw2_pair)
    b_far = shift(b_foll, "z", -1)
    near_pair = swap_column(a_near)
    far_out, near_pair = hold(a_far, near_pair)
    far_pair = swap_column(far_out)
    left_out, _ = hold(left, a_far)
    w1_pair, near_pair, sw1_pair, sw2_pair = hold(w1_pair, near_pair, sw1_pair, sw2_pair)
    left_pair = swap_blocks(left_out)
    right_out, _ = hold(right, b_prev)
    right_pair = swap_blocks(right_out)
    w1 = jnp.concatenate([group_w1[0], w1_pair], axis=1)
    b1 = jnp.concatenate([group_b1[0], b1_pair])
    early = jnp.concatenate([a_near, a_far, b_own, b_foll, b_prev, near_pair], axis=0)
    late = jnp.concatenate([far_pair, b_far], axis=0)

    def first(rows):
        return down(jax.nn.relu(jnp.dot(rows, w1, preferred_element_type=jnp.float32) + b1))

    hidden = jnp.concatenate([first(early), first(late)], axis=0)

    def second(hidden, weight, weight_pair):
        weight = jnp.concatenate([weight, weight_pair], axis=0)
        return down(jnp.dot(hidden, weight, preferred_element_type=jnp.float32))

    def block(part, step):
        at = {"own": (0, 4, 10, 5), "prev": (1, 8, 11, 9), "foll": (2, 6, 12, 7), "far": (3, 14, 13, 15)}
        return jnp.concatenate([part[i * count : (i + 1) * count] for i in at[step]], axis=0)

    wide = 4 * count

    def ring(weight, weight_pair, hidden, way, after):
        part = second(hidden, weight, weight_pair)
        own, prev, foll = (block(part, step) for step in ("own", "prev", "foll"))
        via = shift(block(part, "far"), "z", -way)
        if way == 1:
            foll = shift(foll, "z", 1)
            via, foll, after = hold(via, foll, after)
            prev = down(up(prev) + up(via))
            hidden, prev = hold(hidden, prev)
            prev = shift(prev, "z", -1)
        else:
            prev = shift(prev, "z", -1)
            via, after = hold(via, after)
            foll = shift(down(up(foll) + up(via)), "z", 1)
        return up(own) + up(prev) + up(foll), hidden, after

    sum_l, hidden, right_pair = ring(left, left_pair, hidden, 1, right_pair)
    out_l = down(sum_l[2 * count :])
    back_l = swap_column(out_l)
    part = second(hidden, right, right_pair)
    back = swap_column(part[10 * count : 14 * count])
    via = shift(part[14 * count :], "z", 1)
    prev = shift(part[8 * count : 10 * count], "z", -1)
    foll = shift(down(up(part[6 * count : 8 * count]) + up(via)), "z", 1)
    sum_b = up(part[4 * count : 6 * count]) + up(prev) + up(foll)
    back_b = swap_column(down(sum_b[count:]))
    own, prev, foll, far = jnp.split(down(up(part[:wide]) + up(back)), 4)
    via = shift(far, "z", -1)
    foll = shift(foll, "z", 1)
    via, foll = hold(via, foll)
    prev = shift(down(up(prev) + up(via)), "z", -1)
    prev, back_b, back_l = hold(prev, back_b, back_l)
    sum_b = sum_b[:count] + up(back_b)
    sum_l = down(sum_l[: 2 * count] + up(back_l))
    sum_a = up(own) + up(prev) + up(foll)
    sum_r = down(jnp.concatenate([sum_a, sum_b], axis=0))
    returned = exchange(jnp.concatenate([sum_l, sum_r], axis=1))
    group_out = lax.dot_general(
        dispatch_map, returned, (((0,), (0,)), ((), ())), preferred_element_type=jnp.float32
    )
    group_bias = pick(group_of, group_b2)
    middle = residual_in + group_out + group_bias
    shared_in = layer_norm(middle, shared_gain).astype(bf16)

    def shared_first(block):
        return tuple(
            down(jax.nn.relu(jnp.dot(block, w, preferred_element_type=jnp.float32) + b))
            for w, b in ((shared_w1, shared_b1), (sw1_pair, sb1_pair))
        )

    def shared_second(hidden):
        return down(
            jnp.dot(hidden[0], shared_w2, preferred_element_type=jnp.float32)
            + jnp.dot(hidden[1], sw2_pair, preferred_element_type=jnp.float32)
        )

    half_tok = tok_dev // 2
    one, two = shared_in[:half_tok], shared_in[half_tok:]
    prev, foll = shift(one, "y", 1), shift(one, "y", -1)
    far = shift(prev, "y", 1)
    first = jnp.concatenate([one, prev, foll, far], axis=0)
    held, _, _ = hold(two, prev, foll)
    foll = shift(held, "y", -1)
    held, _ = hold(two, far)
    prev = shift(held, "y", 1)
    far = shift(foll, "y", -1)
    other = jnp.concatenate([two, prev, foll, far], axis=0)
    *hidden, _ = hold(*shared_first(first), foll)
    own, prev, foll, via = jnp.split(shared_second(hidden), 4)
    via = shift(via, "y", -1)
    foll = shift(foll, "y", 1)
    prev = down(up(prev) + up(via))
    *hidden, prev_out, foll = hold(*shared_first(other), prev, foll)
    first = up(own) + up(shift(prev_out, "y", -1)) + up(foll)
    other = ring_scatter(*jnp.split(shared_second(hidden), 4), "y", -1)
    shared_out = jnp.concatenate([first, other], axis=0)
    return (middle + shared_out + shared_b2).astype(bf16)


def solution(mesh):
    chips = Mesh(mesh.devices.reshape(4, 2, 4, 2, 2), ("y", "core", "z", "xh", "xl"))
    group = ("y", "core")
    within = ("z", "xh", "xl")
    both = group + within
    placed = (
        P(both, None),
        P(both),
        P(),
        P(),
        P(group, None, within),
        P(group, within),
        P(group, within, None),
        P(),
        P(),
        P(None, group),
        P(group),
        P(group, None),
        P(),
    )
    return jax.shard_map(
        on_device,
        mesh=chips,
        in_specs=placed,
        out_specs=P(both, None),
        check_vma=False,
    )
```

```python
import jax
import jax.numpy as jnp
from jax import lax
from jax.experimental import pallas as pl
from jax.experimental.pallas import tpu as pltpu
from jax.sharding import Mesh, PartitionSpec as P

X = ("xh", "xl")


def layer_norm(values, gains):
    centre = jnp.mean(values, axis=-1, keepdims=True)
    centred = values - centre
    spread = jnp.mean(centred * centred, axis=-1, keepdims=True)
    return centred * lax.rsqrt(spread + 1e-05) * gains


def shift(value, axis, step):
    size = lax.axis_size(axis)
    return lax.ppermute(value, axis, [(i, (i + step) % size) for i in range(size)])


def swap_column(value):
    return lax.ppermute(value, "xl", [(0, 1), (1, 0)])


def swap_blocks(value):
    return lax.ppermute(value, X, [(0, 3), (3, 0), (1, 2), (2, 1)])


def swap_core(value):
    return lax.ppermute(value, "core", [(0, 1), (1, 0)])


def up(value):
    return value.astype(jnp.float32)


def down(value):
    return value.astype(jnp.bfloat16)


def hold(*values):
    return lax.optimization_barrier(values)


def ring_scatter(own, prev, foll, far, axis, way):
    via = up(shift(far, axis, -way))
    if way == 1:
        prev = down(up(prev) + via)
    else:
        foll = down(up(foll) + via)
    return up(own) + up(shift(prev, axis, -1)) + up(shift(foll, axis, 1))


def dispatch(tokens, group_of, group_gain, capacity):
    num_tok, width = tokens.shape
    num_groups = group_gain.shape[0]
    num_slots = num_groups * capacity

    def body(tokens_ref, group_ref, gain_ref, out_ref, position_ref, rows_ref):
        group = group_ref[...]
        member = (lax.broadcasted_iota(jnp.int32, (num_groups, num_tok), 0) == group).astype(
            jnp.float32
        )
        before = (
            lax.broadcasted_iota(jnp.int32, (num_tok, num_tok), 0)
            < lax.broadcasted_iota(jnp.int32, (num_tok, num_tok), 1)
        ).astype(jnp.float32)
        earlier = jnp.dot(
            member.astype(jnp.bfloat16),
            before.astype(jnp.bfloat16),
            preferred_element_type=jnp.float32,
        )
        slot = jnp.sum(earlier * member, axis=0, keepdims=True)
        position = group * capacity + slot.astype(jnp.int32)
        position_ref[...] = position
        chosen = lax.broadcasted_iota(jnp.int32, (num_slots, num_tok), 0) == position
        rows_ref[...] = jnp.dot(
            chosen.astype(jnp.float32).astype(jnp.bfloat16),
            tokens_ref[...],
            preferred_element_type=jnp.float32,
        )
        for start in range(0, num_slots, 16):
            rows = rows_ref[start : start + 16]
            gains = [
                jnp.broadcast_to(gain_ref[at // capacity : at // capacity + 1], (8, width))
                for at in (start, start + 8)
            ]
            normed = layer_norm(rows, jnp.concatenate(gains, axis=0))
            out_ref[start : start + 16] = normed.astype(jnp.bfloat16)

    outgoing, position = pl.pallas_call(
        body,
        in_specs=[pl.BlockSpec(memory_space=pltpu.VMEM)] * 3,
        out_specs=[pl.BlockSpec(memory_space=pltpu.VMEM)] * 2,
        out_shape=[
            jax.ShapeDtypeStruct((num_slots, width), jnp.bfloat16),
            jax.ShapeDtypeStruct((1, num_tok), jnp.int32),
        ],
        scratch_shapes=[pltpu.VMEM((num_slots, width), jnp.float32)],
        compiler_params=pltpu.CompilerParams(vmem_limit_bytes=16 * 1024 * 1024),
        name="dispatch",
    )(tokens, group_of.reshape(1, num_tok), group_gain)
    return outgoing, position[0]


def on_chip(value):
    def copy(source, target):
        pltpu.sync_copy(source, target)

    return pl.pallas_call(
        copy,
        in_specs=[pl.BlockSpec(memory_space=pl.ANY)],
        out_specs=pl.BlockSpec(memory_space=pltpu.VMEM),
        out_shape=pltpu.VMEM(value.shape, value.dtype),
        compiler_params=pltpu.CompilerParams(vmem_limit_bytes=262144),
        name="on_chip",
    )(value)


def pick(index, table):
    rows = jnp.broadcast_to(table[0], (index.shape[0], table.shape[1]))
    for i in range(1, table.shape[0]):
        rows = jnp.where((index == i)[:, None], table[i], rows)
    return rows


def on_device(
    tokens,
    languages,
    lang_group,
    group_gain,
    group_w1,
    group_b1,
    group_w2,
    group_b2,
    shared_gain,
    shared_w1,
    shared_b1,
    shared_w2,
    shared_b2,
):
    tok_dev = tokens.shape[0]
    width_model = tokens.shape[1]
    num_groups = group_gain.shape[0]
    num_langs = lang_group.shape[0]
    capacity = 3 * tok_dev // (2 * num_groups)
    bf16 = jnp.bfloat16

    cut = width_model // 2
    left, right = group_w2[0, :, :cut], group_w2[0, :, cut:]
    w1_out, b1_pair = hold(group_w1[0], swap_blocks(group_b1[0]))
    w1_pair = swap_blocks(w1_out)

    residual_in = tokens.astype(jnp.float32)
    lang_hit = (languages[:, None] == jnp.arange(num_langs, dtype=jnp.int32)[None, :]).astype(
        jnp.int32
    )
    group_of = jnp.sum(lang_hit * lang_group[None, :], axis=1)
    outgoing, position = dispatch(tokens, group_of, group_gain, capacity)
    dispatch_map = (
        position[None, :] == jnp.arange(num_groups * capacity, dtype=jnp.int32)[:, None]
    ).astype(bf16)
    count = num_groups * capacity // 2

    def exchange(value):
        value = value.reshape(num_groups, capacity, value.shape[-1])
        value = lax.all_to_all(value, ("y", "core"), split_axis=0, concat_axis=0, tiled=True)
        return value.reshape(2 * count, value.shape[-1])

    arrived, sw1_pair, sw2_pair, sb1_pair = hold(
        exchange(outgoing), swap_core(shared_w1), swap_core(shared_w2), swap_core(shared_b1)
    )
    a_own, b_own = arrived[:count], arrived[count:]
    a_prev, a_foll = shift(a_own, "z", 1), shift(a_own, "z", -1)
    a_far = shift(a_prev, "z", 1)
    b_pair = swap_column(b_own)
    a_near = jnp.concatenate([a_own, a_prev, a_foll], axis=0)
    a_near, b_pair = hold(a_near, b_pair)
    (b_own,) = hold(jnp.concatenate([b_own, b_pair], axis=0))
    b_foll = shift(b_own, "z", -1)
    held, a_far = hold(b_own, a_far)
    b_prev = shift(held, "z", 1)
    sw1_pair, sw2_pair, _ = hold(sw1_pair, sw2_pair, b_own)
    sw1_pair, sw2_pair = on_chip(sw1_pair), on_chip(sw2_pair)
    b_far = shift(b_foll, "z", -1)
    near_pair = swap_column(a_near)
    far_out, near_pair = hold(a_far, near_pair)
    far_pair = swap_column(far_out)
    left_out, _ = hold(left, a_far)
    w1_pair, near_pair, sw1_pair, sw2_pair = hold(w1_pair, near_pair, sw1_pair, sw2_pair)
    left_pair = swap_blocks(left_out)
    right_out, _ = hold(right, b_prev)
    right_pair = swap_blocks(right_out)
    w1 = jnp.concatenate([group_w1[0], w1_pair], axis=1)
    b1 = jnp.concatenate([group_b1[0], b1_pair])
    early = jnp.concatenate([a_near, a_far, b_own, b_foll, b_prev, near_pair], axis=0)
    late = jnp.concatenate([far_pair, b_far], axis=0)

    def first(rows):
        return down(jax.nn.relu(jnp.dot(rows, w1, preferred_element_type=jnp.float32) + b1))

    hidden = jnp.concatenate([first(early), first(late)], axis=0)

    def second(hidden, weight, weight_pair):
        weight = jnp.concatenate([weight, weight_pair], axis=0)
        return down(jnp.dot(hidden, weight, preferred_element_type=jnp.float32))

    def block(part, step):
        at = {"own": (0, 4, 10, 5), "prev": (1, 8, 11, 9), "foll": (2, 6, 12, 7), "far": (3, 14, 13, 15)}
        return jnp.concatenate([part[i * count : (i + 1) * count] for i in at[step]], axis=0)

    wide = 4 * count

    part = second(hidden, left, left_pair)
    own, prev, foll = (block(part, step) for step in ("own", "prev", "foll"))
    via = shift(block(part, "far"), "z", -1)
    foll = shift(foll, "z", 1)
    part = second(hidden, right, right_pair)
    via, foll, _ = hold(via, foll, part)
    prev = shift(down(up(prev) + up(via)), "z", -1)
    sum_l = up(own) + up(prev) + up(foll)
    back_l = swap_column(down(sum_l[2 * count :]))

    back = swap_column(part[10 * count : 14 * count])
    via = shift(part[14 * count :], "z", 1)
    prev = shift(part[8 * count : 10 * count], "z", -1)
    foll = shift(down(up(part[6 * count : 8 * count]) + up(via)), "z", 1)
    sum_b = up(part[4 * count : 6 * count]) + up(prev) + up(foll)
    back_b = swap_column(down(sum_b[count:]))
    own, prev, foll, far = jnp.split(down(up(part[:wide]) + up(back)), 4)
    via = shift(far, "z", -1)
    foll = shift(foll, "z", 1)
    prev = shift(down(up(prev) + up(via)), "z", -1)
    prev, foll, back_b, back_l = hold(prev, foll, back_b, back_l)
    sum_b = sum_b[:count] + up(back_b)
    sum_l = down(sum_l[: 2 * count] + up(back_l))
    sum_a = up(own) + up(prev) + up(foll)
    sum_r = down(jnp.concatenate([sum_a, sum_b], axis=0))
    returned = exchange(jnp.concatenate([sum_l, sum_r], axis=1))
    group_out = lax.dot_general(
        dispatch_map, returned, (((0,), (0,)), ((), ())), preferred_element_type=jnp.float32
    )
    group_bias = pick(group_of, group_b2)
    middle = residual_in + group_out + group_bias
    shared_in = layer_norm(middle, shared_gain).astype(bf16)

    def shared_first(block):
        return tuple(
            down(jax.nn.relu(jnp.dot(block, w, preferred_element_type=jnp.float32) + b))
            for w, b in ((shared_w1, shared_b1), (sw1_pair, sb1_pair))
        )

    def shared_second(hidden):
        return down(
            jnp.dot(hidden[0], shared_w2, preferred_element_type=jnp.float32)
            + jnp.dot(hidden[1], sw2_pair, preferred_element_type=jnp.float32)
        )

    half_tok = tok_dev // 2
    one, two = shared_in[:half_tok], shared_in[half_tok:]
    prev, foll = shift(one, "y", 1), shift(one, "y", -1)
    far = shift(prev, "y", 1)
    first = jnp.concatenate([one, prev, foll, far], axis=0)
    held, _, _ = hold(two, prev, foll)
    foll = shift(held, "y", -1)
    held, _ = hold(two, far)
    prev = shift(held, "y", 1)
    far = shift(foll, "y", -1)
    other = jnp.concatenate([two, prev, foll, far], axis=0)
    *hidden, _ = hold(*shared_first(first), foll)
    own, prev, foll, via = jnp.split(shared_second(hidden), 4)
    via = shift(via, "y", -1)
    foll = shift(foll, "y", 1)
    prev = down(up(prev) + up(via))
    *hidden, prev_out, foll = hold(*shared_first(other), prev, foll)
    first = up(own) + up(shift(prev_out, "y", -1)) + up(foll)
    other = ring_scatter(*jnp.split(shared_second(hidden), 4), "y", -1)
    shared_out = jnp.concatenate([first, other], axis=0)
    return (middle + shared_out + shared_b2).astype(bf16)


def solution(mesh):
    chips = Mesh(mesh.devices.reshape(4, 2, 4, 2, 2), ("y", "core", "z", "xh", "xl"))
    group = ("y", "core")
    within = ("z", "xh", "xl")
    both = group + within
    placed = (
        P(both, None),
        P(both),
        P(),
        P(),
        P(group, None, within),
        P(group, within),
        P(group, within, None),
        P(),
        P(),
        P(None, group),
        P(group),
        P(group, None),
        P(),
    )
    return jax.shard_map(
        on_device,
        mesh=chips,
        in_specs=placed,
        out_specs=P(both, None),
        check_vma=False,
    )
```

```python
import jax
import jax.numpy as jnp
from jax import lax
from jax.experimental import pallas as pl
from jax.experimental.pallas import tpu as pltpu
from jax.sharding import Mesh, PartitionSpec as P

X = ("xh", "xl")


def layer_norm(values, gains):
    centre = jnp.mean(values, axis=-1, keepdims=True)
    centred = values - centre
    spread = jnp.mean(centred * centred, axis=-1, keepdims=True)
    return centred * lax.rsqrt(spread + 1e-05) * gains


def shift(value, axis, step):
    size = lax.axis_size(axis)
    return lax.ppermute(value, axis, [(i, (i + step) % size) for i in range(size)])


def swap_column(value):
    return lax.ppermute(value, "xl", [(0, 1), (1, 0)])


def swap_blocks(value):
    return lax.ppermute(value, X, [(0, 3), (3, 0), (1, 2), (2, 1)])


def swap_core(value):
    return lax.ppermute(value, "core", [(0, 1), (1, 0)])


def up(value):
    return value.astype(jnp.float32)


def down(value):
    return value.astype(jnp.bfloat16)


def hold(*values):
    return lax.optimization_barrier(values)


def ring_scatter(own, prev, foll, far, axis, way):
    via = up(shift(far, axis, -way))
    if way == 1:
        prev = down(up(prev) + via)
    else:
        foll = down(up(foll) + via)
    return up(own) + up(shift(prev, axis, -1)) + up(shift(foll, axis, 1))


def dispatch(tokens, group_of, group_gain, capacity):
    num_tok, width = tokens.shape
    num_groups = group_gain.shape[0]
    num_slots = num_groups * capacity

    def body(tokens_ref, group_ref, gain_ref, out_ref, position_ref, rows_ref):
        group = group_ref[...]
        member = (lax.broadcasted_iota(jnp.int32, (num_groups, num_tok), 0) == group).astype(
            jnp.float32
        )
        before = (
            lax.broadcasted_iota(jnp.int32, (num_tok, num_tok), 0)
            < lax.broadcasted_iota(jnp.int32, (num_tok, num_tok), 1)
        ).astype(jnp.float32)
        earlier = jnp.dot(
            member.astype(jnp.bfloat16),
            before.astype(jnp.bfloat16),
            preferred_element_type=jnp.float32,
        )
        slot = jnp.sum(earlier * member, axis=0, keepdims=True)
        position = group * capacity + slot.astype(jnp.int32)
        position_ref[...] = position
        chosen = lax.broadcasted_iota(jnp.int32, (num_slots, num_tok), 0) == position
        rows_ref[...] = jnp.dot(
            chosen.astype(jnp.float32).astype(jnp.bfloat16),
            tokens_ref[...],
            preferred_element_type=jnp.float32,
        )
        for start in range(0, num_slots, 16):
            rows = rows_ref[start : start + 16]
            gains = [
                jnp.broadcast_to(gain_ref[at // capacity : at // capacity + 1], (8, width))
                for at in (start, start + 8)
            ]
            normed = layer_norm(rows, jnp.concatenate(gains, axis=0))
            out_ref[start : start + 16] = normed.astype(jnp.bfloat16)

    outgoing, position = pl.pallas_call(
        body,
        in_specs=[pl.BlockSpec(memory_space=pltpu.VMEM)] * 3,
        out_specs=[pl.BlockSpec(memory_space=pltpu.VMEM)] * 2,
        out_shape=[
            jax.ShapeDtypeStruct((num_slots, width), jnp.bfloat16),
            jax.ShapeDtypeStruct((1, num_tok), jnp.int32),
        ],
        scratch_shapes=[pltpu.VMEM((num_slots, width), jnp.float32)],
        compiler_params=pltpu.CompilerParams(vmem_limit_bytes=16 * 1024 * 1024),
        name="dispatch",
    )(tokens, group_of.reshape(1, num_tok), group_gain)
    return outgoing, position[0]


def on_chip(value):
    def copy(source, target):
        pltpu.sync_copy(source, target)

    return pl.pallas_call(
        copy,
        in_specs=[pl.BlockSpec(memory_space=pl.ANY)],
        out_specs=pl.BlockSpec(memory_space=pltpu.VMEM),
        out_shape=pltpu.VMEM(value.shape, value.dtype),
        compiler_params=pltpu.CompilerParams(vmem_limit_bytes=262144),
        name="on_chip",
    )(value)


def pick(index, table):
    rows = jnp.broadcast_to(table[0], (index.shape[0], table.shape[1]))
    for i in range(1, table.shape[0]):
        rows = jnp.where((index == i)[:, None], table[i], rows)
    return rows


def on_device(
    tokens,
    languages,
    lang_group,
    group_gain,
    group_w1,
    group_b1,
    group_w2,
    group_b2,
    shared_gain,
    shared_w1,
    shared_b1,
    shared_w2,
    shared_b2,
):
    tok_dev = tokens.shape[0]
    width_model = tokens.shape[1]
    num_groups = group_gain.shape[0]
    num_langs = lang_group.shape[0]
    capacity = 3 * tok_dev // (2 * num_groups)
    bf16 = jnp.bfloat16

    cut = width_model // 2
    left, right = group_w2[0, :, :cut], group_w2[0, :, cut:]
    w1_out, b1_pair = hold(group_w1[0], swap_blocks(group_b1[0]))
    w1_pair = swap_blocks(w1_out)

    residual_in = tokens.astype(jnp.float32)
    lang_hit = (languages[:, None] == jnp.arange(num_langs, dtype=jnp.int32)[None, :]).astype(
        jnp.int32
    )
    group_of = jnp.sum(lang_hit * lang_group[None, :], axis=1)
    outgoing, position = dispatch(tokens, group_of, group_gain, capacity)
    dispatch_map = (
        position[None, :] == jnp.arange(num_groups * capacity, dtype=jnp.int32)[:, None]
    ).astype(bf16)
    count = num_groups * capacity // 2

    def exchange(value):
        value = value.reshape(num_groups, capacity, value.shape[-1])
        value = lax.all_to_all(value, ("y", "core"), split_axis=0, concat_axis=0, tiled=True)
        return value.reshape(2 * count, value.shape[-1])

    arrived, sw1_pair, sw2_pair, sb1_pair = hold(
        exchange(outgoing), swap_core(shared_w1), swap_core(shared_w2), swap_core(shared_b1)
    )
    a_own, b_own = arrived[:count], arrived[count:]
    a_prev, a_foll = shift(a_own, "z", 1), shift(a_own, "z", -1)
    a_far = shift(a_prev, "z", 1)
    b_pair = swap_column(b_own)
    a_near = jnp.concatenate([a_own, a_prev, a_foll], axis=0)
    a_near, b_pair = hold(a_near, b_pair)
    (b_own,) = hold(jnp.concatenate([b_own, b_pair], axis=0))
    b_foll = shift(b_own, "z", -1)
    held, a_far = hold(b_own, a_far)
    b_prev = shift(held, "z", 1)
    sw1_pair, sw2_pair, _ = hold(sw1_pair, sw2_pair, b_own)
    sw1_pair, sw2_pair = on_chip(sw1_pair), on_chip(sw2_pair)
    b_far = shift(b_foll, "z", -1)
    near_pair = swap_column(a_near)
    far_out, near_pair = hold(a_far, near_pair)
    far_pair = swap_column(far_out)
    left_out, _ = hold(left, a_far)
    w1_pair, near_pair, sw1_pair, sw2_pair = hold(w1_pair, near_pair, sw1_pair, sw2_pair)
    left_pair = swap_blocks(left_out)
    right_out, _ = hold(right, b_prev)
    right_pair = swap_blocks(right_out)
    w1 = jnp.concatenate([group_w1[0], w1_pair], axis=1)
    b1 = jnp.concatenate([group_b1[0], b1_pair])
    early = jnp.concatenate([a_near, a_far, b_own, b_foll, b_prev, near_pair], axis=0)
    late = jnp.concatenate([far_pair, b_far], axis=0)

    def first(rows):
        return down(jax.nn.relu(jnp.dot(rows, w1, preferred_element_type=jnp.float32) + b1))

    hidden = jnp.concatenate([first(early), first(late)], axis=0)

    def second(hidden, weight, weight_pair):
        weight = jnp.concatenate([weight, weight_pair], axis=0)
        return down(jnp.dot(hidden, weight, preferred_element_type=jnp.float32))

    def block(part, step):
        at = {"own": (0, 4, 10, 5), "prev": (1, 8, 11, 9), "foll": (2, 6, 12, 7), "far": (3, 14, 13, 15)}
        return jnp.concatenate([part[i * count : (i + 1) * count] for i in at[step]], axis=0)

    wide = 4 * count

    part = second(hidden, left, left_pair)
    own, prev, foll = (block(part, step) for step in ("own", "prev", "foll"))
    via = shift(block(part, "far"), "z", -1)
    foll = shift(foll, "z", 1)
    part = second(hidden, right, right_pair)
    via, foll, _ = hold(via, foll, part)
    prev = shift(down(up(prev) + up(via)), "z", -1)
    sum_l = up(own) + up(prev) + up(foll)
    back_l = swap_column(down(sum_l[2 * count :]))

    back = swap_column(part[10 * count : 14 * count])
    via = shift(part[14 * count :], "z", 1)
    prev = shift(part[8 * count : 10 * count], "z", -1)
    foll = shift(down(up(part[6 * count : 8 * count]) + up(via)), "z", 1)
    sum_b = up(part[4 * count : 6 * count]) + up(prev) + up(foll)
    back_b = swap_column(down(sum_b[count:]))
    own, prev, foll, far = jnp.split(down(up(part[:wide]) + up(back)), 4)
    via = shift(far, "z", 1)
    prev = shift(prev, "z", -1)
    foll = shift(down(up(foll) + up(via)), "z", 1)
    prev, foll, back_b, back_l = hold(prev, foll, back_b, back_l)
    sum_b = sum_b[:count] + up(back_b)
    sum_l = down(sum_l[: 2 * count] + up(back_l))
    sum_a = up(own) + up(prev) + up(foll)
    sum_r = down(jnp.concatenate([sum_a, sum_b], axis=0))
    returned = exchange(jnp.concatenate([sum_l, sum_r], axis=1))
    group_out = lax.dot_general(
        dispatch_map, returned, (((0,), (0,)), ((), ())), preferred_element_type=jnp.float32
    )
    group_bias = pick(group_of, group_b2)
    middle = residual_in + group_out + group_bias
    shared_in = layer_norm(middle, shared_gain).astype(bf16)

    def shared_first(block):
        return tuple(
            down(jax.nn.relu(jnp.dot(block, w, preferred_element_type=jnp.float32) + b))
            for w, b in ((shared_w1, shared_b1), (sw1_pair, sb1_pair))
        )

    def shared_second(hidden):
        return down(
            jnp.dot(hidden[0], shared_w2, preferred_element_type=jnp.float32)
            + jnp.dot(hidden[1], sw2_pair, preferred_element_type=jnp.float32)
        )

    half_tok = tok_dev // 2
    one, two = shared_in[:half_tok], shared_in[half_tok:]
    prev, foll = shift(one, "y", 1), shift(one, "y", -1)
    far = shift(prev, "y", 1)
    first = jnp.concatenate([one, prev, foll, far], axis=0)
    held, _, _ = hold(two, prev, foll)
    foll = shift(held, "y", -1)
    held, _ = hold(two, far)
    prev = shift(held, "y", 1)
    far = shift(foll, "y", -1)
    other = jnp.concatenate([two, prev, foll, far], axis=0)
    *hidden, _ = hold(*shared_first(first), foll)
    own, prev, foll, via = jnp.split(shared_second(hidden), 4)
    via = shift(via, "y", -1)
    foll = shift(foll, "y", 1)
    prev = down(up(prev) + up(via))
    *hidden, prev_out, foll = hold(*shared_first(other), prev, foll)
    first = up(own) + up(shift(prev_out, "y", -1)) + up(foll)
    other = ring_scatter(*jnp.split(shared_second(hidden), 4), "y", -1)
    shared_out = jnp.concatenate([first, other], axis=0)
    return (middle + shared_out + shared_b2).astype(bf16)


def solution(mesh):
    chips = Mesh(mesh.devices.reshape(4, 2, 4, 2, 2), ("y", "core", "z", "xh", "xl"))
    group = ("y", "core")
    within = ("z", "xh", "xl")
    both = group + within
    placed = (
        P(both, None),
        P(both),
        P(),
        P(),
        P(group, None, within),
        P(group, within),
        P(group, within, None),
        P(),
        P(),
        P(None, group),
        P(group),
        P(group, None),
        P(),
    )
    return jax.shard_map(
        on_device,
        mesh=chips,
        in_specs=placed,
        out_specs=P(both, None),
        check_vma=False,
    )
```

```python
import jax
import jax.numpy as jnp
from jax import lax
from jax.experimental import pallas as pl
from jax.experimental.pallas import tpu as pltpu
from jax.sharding import Mesh, PartitionSpec as P

X = ("xh", "xl")


def layer_norm(values, gains):
    centre = jnp.mean(values, axis=-1, keepdims=True)
    centred = values - centre
    spread = jnp.mean(centred * centred, axis=-1, keepdims=True)
    return centred * lax.rsqrt(spread + 1e-05) * gains


def shift(value, axis, step):
    size = lax.axis_size(axis)
    return lax.ppermute(value, axis, [(i, (i + step) % size) for i in range(size)])


def swap_column(value):
    return lax.ppermute(value, "xl", [(0, 1), (1, 0)])


def swap_blocks(value):
    return lax.ppermute(value, X, [(0, 3), (3, 0), (1, 2), (2, 1)])


def swap_core(value):
    return lax.ppermute(value, "core", [(0, 1), (1, 0)])


def up(value):
    return value.astype(jnp.float32)


def down(value):
    return value.astype(jnp.bfloat16)


def hold(*values):
    return lax.optimization_barrier(values)


def ring_scatter(own, prev, foll, far, axis, way):
    via = up(shift(far, axis, -way))
    if way == 1:
        prev = down(up(prev) + via)
    else:
        foll = down(up(foll) + via)
    return up(own) + up(shift(prev, axis, -1)) + up(shift(foll, axis, 1))


def dispatch(tokens, group_of, group_gain, capacity):
    num_tok, width = tokens.shape
    num_groups = group_gain.shape[0]
    num_slots = num_groups * capacity

    def body(tokens_ref, group_ref, gain_ref, out_ref, position_ref, rows_ref):
        group = group_ref[...]
        member = (lax.broadcasted_iota(jnp.int32, (num_groups, num_tok), 0) == group).astype(
            jnp.float32
        )
        before = (
            lax.broadcasted_iota(jnp.int32, (num_tok, num_tok), 0)
            < lax.broadcasted_iota(jnp.int32, (num_tok, num_tok), 1)
        ).astype(jnp.float32)
        earlier = jnp.dot(
            member.astype(jnp.bfloat16),
            before.astype(jnp.bfloat16),
            preferred_element_type=jnp.float32,
        )
        slot = jnp.sum(earlier * member, axis=0, keepdims=True)
        position = group * capacity + slot.astype(jnp.int32)
        position_ref[...] = position
        chosen = lax.broadcasted_iota(jnp.int32, (num_slots, num_tok), 0) == position
        rows_ref[...] = jnp.dot(
            chosen.astype(jnp.float32).astype(jnp.bfloat16),
            tokens_ref[...],
            preferred_element_type=jnp.float32,
        )
        for start in range(0, num_slots, 16):
            rows = rows_ref[start : start + 16]
            gains = [
                jnp.broadcast_to(gain_ref[at // capacity : at // capacity + 1], (8, width))
                for at in (start, start + 8)
            ]
            normed = layer_norm(rows, jnp.concatenate(gains, axis=0))
            out_ref[start : start + 16] = normed.astype(jnp.bfloat16)

    outgoing, position = pl.pallas_call(
        body,
        in_specs=[pl.BlockSpec(memory_space=pltpu.VMEM)] * 3,
        out_specs=[pl.BlockSpec(memory_space=pltpu.VMEM)] * 2,
        out_shape=[
            jax.ShapeDtypeStruct((num_slots, width), jnp.bfloat16),
            jax.ShapeDtypeStruct((1, num_tok), jnp.int32),
        ],
        scratch_shapes=[pltpu.VMEM((num_slots, width), jnp.float32)],
        compiler_params=pltpu.CompilerParams(vmem_limit_bytes=16 * 1024 * 1024),
        name="dispatch",
    )(tokens, group_of.reshape(1, num_tok), group_gain)
    return outgoing, position[0]


def on_chip(value):
    def copy(source, target):
        pltpu.sync_copy(source, target)

    return pl.pallas_call(
        copy,
        in_specs=[pl.BlockSpec(memory_space=pl.ANY)],
        out_specs=pl.BlockSpec(memory_space=pltpu.VMEM),
        out_shape=pltpu.VMEM(value.shape, value.dtype),
        compiler_params=pltpu.CompilerParams(vmem_limit_bytes=262144),
        name="on_chip",
    )(value)


def pick(index, table):
    rows = jnp.broadcast_to(table[0], (index.shape[0], table.shape[1]))
    for i in range(1, table.shape[0]):
        rows = jnp.where((index == i)[:, None], table[i], rows)
    return rows


def on_device(
    tokens,
    languages,
    lang_group,
    group_gain,
    group_w1,
    group_b1,
    group_w2,
    group_b2,
    shared_gain,
    shared_w1,
    shared_b1,
    shared_w2,
    shared_b2,
):
    tok_dev = tokens.shape[0]
    width_model = tokens.shape[1]
    num_groups = group_gain.shape[0]
    num_langs = lang_group.shape[0]
    capacity = 3 * tok_dev // (2 * num_groups)
    bf16 = jnp.bfloat16

    cut = width_model // 2
    left, right = group_w2[0, :, :cut], group_w2[0, :, cut:]
    w1_out, b1_pair = hold(group_w1[0], swap_blocks(group_b1[0]))
    w1_pair = swap_blocks(w1_out)

    residual_in = tokens.astype(jnp.float32)
    lang_hit = (languages[:, None] == jnp.arange(num_langs, dtype=jnp.int32)[None, :]).astype(
        jnp.int32
    )
    group_of = jnp.sum(lang_hit * lang_group[None, :], axis=1)
    outgoing, position = dispatch(tokens, group_of, group_gain, capacity)
    dispatch_map = (
        position[None, :] == jnp.arange(num_groups * capacity, dtype=jnp.int32)[:, None]
    ).astype(bf16)
    count = num_groups * capacity // 2

    def exchange(value):
        value = value.reshape(num_groups, capacity, value.shape[-1])
        value = lax.all_to_all(value, ("y", "core"), split_axis=0, concat_axis=0, tiled=True)
        return value.reshape(2 * count, value.shape[-1])

    arrived, sw1_pair, sw2_pair, sb1_pair = hold(
        exchange(outgoing), swap_core(shared_w1), swap_core(shared_w2), swap_core(shared_b1)
    )
    a_own, b_own = arrived[:count], arrived[count:]
    a_prev, a_foll = shift(a_own, "z", 1), shift(a_own, "z", -1)
    a_far = shift(a_prev, "z", 1)
    b_pair = swap_column(b_own)
    a_near = jnp.concatenate([a_own, a_prev, a_foll], axis=0)
    a_near, b_pair = hold(a_near, b_pair)
    (b_own,) = hold(jnp.concatenate([b_own, b_pair], axis=0))
    b_foll = shift(b_own, "z", -1)
    held, a_far = hold(b_own, a_far)
    b_prev = shift(held, "z", 1)
    sw1_pair, sw2_pair, _ = hold(sw1_pair, sw2_pair, b_own)
    sw1_pair, sw2_pair = on_chip(sw1_pair), on_chip(sw2_pair)
    b_far = shift(b_foll, "z", -1)
    near_pair = swap_column(a_near)
    far_out, near_pair = hold(a_far, near_pair)
    far_pair = swap_column(far_out)
    left_out, _ = hold(left, a_far)
    w1_pair, near_pair, sw1_pair, sw2_pair = hold(w1_pair, near_pair, sw1_pair, sw2_pair)
    left_pair = swap_blocks(left_out)
    right_out, _ = hold(right, b_prev)
    right_pair = swap_blocks(right_out)
    w1 = jnp.concatenate([group_w1[0], w1_pair], axis=1)
    b1 = jnp.concatenate([group_b1[0], b1_pair])
    early = jnp.concatenate([a_near, a_far, b_own, b_foll, b_prev, near_pair], axis=0)
    late = jnp.concatenate([far_pair, b_far], axis=0)

    def first(rows):
        return down(jax.nn.relu(jnp.dot(rows, w1, preferred_element_type=jnp.float32) + b1))

    hidden = jnp.concatenate([first(early), first(late)], axis=0)

    def second(hidden, weight, weight_pair):
        weight = jnp.concatenate([weight, weight_pair], axis=0)
        return down(jnp.dot(hidden, weight, preferred_element_type=jnp.float32))

    def block(part, step):
        at = {"own": (0, 4, 10, 5), "prev": (1, 8, 11, 9), "foll": (2, 6, 12, 7), "far": (3, 14, 13, 15)}
        return jnp.concatenate([part[i * count : (i + 1) * count] for i in at[step]], axis=0)

    wide = 4 * count

    part = second(hidden, left, left_pair)
    own, prev, foll = (block(part, step) for step in ("own", "prev", "foll"))
    via = shift(block(part, "far"), "z", -1)
    foll = shift(foll, "z", 1)
    part = second(hidden, right, right_pair)
    via, foll, _ = hold(via, foll, part)
    added = down(up(prev) + up(via))
    prev = shift(added, "z", -1)
    sum_l = up(own) + up(prev) + up(foll)
    back_l = swap_column(down(sum_l[2 * count :]))

    back = swap_column(part[10 * count : 14 * count])
    via = shift(part[14 * count :], "z", 1)
    held, _ = hold(part[8 * count : 10 * count], added)
    prev = shift(held, "z", -1)
    foll = shift(down(up(part[6 * count : 8 * count]) + up(via)), "z", 1)
    sum_b = up(part[4 * count : 6 * count]) + up(prev) + up(foll)
    back_b = swap_column(down(sum_b[count:]))
    own, prev, foll, far = jnp.split(down(up(part[:wide]) + up(back)), 4)
    via = shift(far, "z", 1)
    prev = shift(prev, "z", -1)
    foll = shift(down(up(foll) + up(via)), "z", 1)
    prev, foll, back_b, back_l = hold(prev, foll, back_b, back_l)
    sum_b = sum_b[:count] + up(back_b)
    sum_l = down(sum_l[: 2 * count] + up(back_l))
    sum_a = up(own) + up(prev) + up(foll)
    sum_r = down(jnp.concatenate([sum_a, sum_b], axis=0))
    returned = exchange(jnp.concatenate([sum_l, sum_r], axis=1))
    group_out = lax.dot_general(
        dispatch_map, returned, (((0,), (0,)), ((), ())), preferred_element_type=jnp.float32
    )
    group_bias = pick(group_of, group_b2)
    middle = residual_in + group_out + group_bias
    shared_in = layer_norm(middle, shared_gain).astype(bf16)

    def shared_first(block):
        return tuple(
            down(jax.nn.relu(jnp.dot(block, w, preferred_element_type=jnp.float32) + b))
            for w, b in ((shared_w1, shared_b1), (sw1_pair, sb1_pair))
        )

    def shared_second(hidden):
        return down(
            jnp.dot(hidden[0], shared_w2, preferred_element_type=jnp.float32)
            + jnp.dot(hidden[1], sw2_pair, preferred_element_type=jnp.float32)
        )

    half_tok = tok_dev // 2
    one, two = shared_in[:half_tok], shared_in[half_tok:]
    prev, foll = shift(one, "y", 1), shift(one, "y", -1)
    far = shift(prev, "y", 1)
    first = jnp.concatenate([one, prev, foll, far], axis=0)
    held, _, _ = hold(two, prev, foll)
    foll = shift(held, "y", -1)
    held, _ = hold(two, far)
    prev = shift(held, "y", 1)
    far = shift(foll, "y", -1)
    other = jnp.concatenate([two, prev, foll, far], axis=0)
    *hidden, _ = hold(*shared_first(first), foll)
    own, prev, foll, via = jnp.split(shared_second(hidden), 4)
    via = shift(via, "y", -1)
    foll = shift(foll, "y", 1)
    prev = down(up(prev) + up(via))
    *hidden, prev_out, foll = hold(*shared_first(other), prev, foll)
    first = up(own) + up(shift(prev_out, "y", -1)) + up(foll)
    other = ring_scatter(*jnp.split(shared_second(hidden), 4), "y", -1)
    shared_out = jnp.concatenate([first, other], axis=0)
    return (middle + shared_out + shared_b2).astype(bf16)


def solution(mesh):
    chips = Mesh(mesh.devices.reshape(4, 2, 4, 2, 2), ("y", "core", "z", "xh", "xl"))
    group = ("y", "core")
    within = ("z", "xh", "xl")
    both = group + within
    placed = (
        P(both, None),
        P(both),
        P(),
        P(),
        P(group, None, within),
        P(group, within),
        P(group, within, None),
        P(),
        P(),
        P(None, group),
        P(group),
        P(group, None),
        P(),
    )
    return jax.shard_map(
        on_device,
        mesh=chips,
        in_specs=placed,
        out_specs=P(both, None),
        check_vma=False,
    )
```
